32 devices in a mesh: curve: 32 (over z, y, x, core).
Axes of the slice: x: 2, y: 2, z: 4, core: 2. Of those that a mesh axis runs over, the one named last changes fastest.
Arguments:
- multipole: bfloat16 [152, 32768], P(None, 'curve'), may hold values from -6 to 6
- upward_maps: bfloat16 [8, 152, 152], replicated, may hold values from -0.15625 to 0.15625
- transfer_maps: bfloat16 [316, 152, 152], replicated, may hold values from -0.03125 to 0.03125
- downward_maps: bfloat16 [8, 152, 152], replicated, may hold values from -0.5 to 0.5
- check_inverse: bfloat16 [152, 152], replicated, may hold values from -0.5 to 0.5
- fine_lists: int32 [316, 32768], P(None, 'curve'), may hold values from -1 to 1023, as said below
- coarse_lists: int32 [316, 4096], P(None, 'curve'), may hold values from -1 to 127, as said below
Outputs:
- local_density: bfloat16 [152, 32768], P(None, 'curve')
The draws below stay inside these ranges and needn't reach their ends.
Inputs may be any that keep to these rules, and one draw needn't show every extreme that they name: `fine_lists`: entry k of box t is -1 or the place, within its own brick, of the fine box at offset k from t; it is a place only where that box lies in the grid, its parent touches the parent of t, and both boxes are present in the tree. `coarse_lists`: entry k of box t is -1 or the place, within its own brick, of the coarse box at offset k from t; it is a place only where that box lies in the grid, its parent touches the parent of t, and both boxes are present in the tree (a coarse box is present when one of its children is).
All inputs are finite; a program needn't handle non-finite values.
Results may differ from the reference program's by a relative error of at most 0.0055.
Values may be sent and summed in bfloat16 or wider, within the bound.
No kernel may reach another device: no remote copies, remote signals or barrier semaphores. Data moves between devices by JAX's collectives and lax.ppermute only.
A program may use at most 704 MiB of HBM per device.

```python
import jax
import jax.numpy as jnp
import numpy as np
from jax import lax

P_SIZE = 152
OFFS = 316
BX = 8
BY = 8
BZ = 16
BOXES = 32768
N_CURVE = 32


SHIFTS = [(first_axis, second_axis, third_axis) for first_axis in range(-3, 4) for second_axis in range(-3, 4) for third_axis in range(-3, 4) if max(abs(first_axis), abs(second_axis), abs(third_axis)) >= 2]


def curve_numbers(brick, devices):
    levels = devices.bit_length() - 1
    limits = (2 ** (levels // 3), 2 ** ((levels + 1) // 3), 2 ** ((levels + 2) // 3))
    numbers = np.arange(devices)
    places = [np.zeros(devices, np.int64) for axis_number in range(3)]
    for bit_place in range(levels):
        places[2 - bit_place % 3] += (numbers >> bit_place & 1) << bit_place // 3
    box_count = brick[0] * brick[1] * brick[2]
    within = np.arange(box_count).reshape(brick)
    numbering = np.zeros((limits[0] * brick[0], limits[1] * brick[1], limits[2] * brick[2]), np.int64)
    for device_number in range(devices):
        corner_x = places[0][device_number] * brick[0]
        corner_y = places[1][device_number] * brick[1]
        corner_z = places[2][device_number] * brick[2]
        numbering[corner_x:corner_x + brick[0], corner_y:corner_y + brick[1], corner_z:corner_z + brick[2]] = device_number * box_count + within
    return numbering


def level_lists(present, numbering, box_count):
    size_x, size_y, size_z = numbering.shape
    padded_present = jnp.pad(present, 3)
    padded_numbers = jnp.pad(jnp.asarray(numbering % box_count, jnp.int32), 3, constant_values=-1)
    coord_lists = (np.arange(size_x)[:, None, None], np.arange(size_y)[None, :, None], np.arange(size_z)[None, None, :])
    rows = []
    for offset in SHIFTS:
        allowed = np.ones(numbering.shape, bool)
        for axis_number in range(3):
            coords = coord_lists[axis_number]
            moved = coords + offset[axis_number]
            allowed = allowed & (moved // 2 - coords // 2 >= -1) & (moved // 2 - coords // 2 <= 1)
        source_present = padded_present[3 + offset[0]:3 + offset[0] + size_x, 3 + offset[1]:3 + offset[1] + size_y, 3 + offset[2]:3 + offset[2] + size_z]
        source_number = padded_numbers[3 + offset[0]:3 + offset[0] + size_x, 3 + offset[1]:3 + offset[1] + size_y, 3 + offset[2]:3 + offset[2] + size_z]
        keeping = jnp.asarray(allowed) & present & source_present
        rows.append(jnp.where(keeping, source_number, -1))
    stacked = jnp.stack(rows).reshape(len(SHIFTS), -1)
    ordering = np.argsort(numbering.ravel())
    return stacked[:, ordering].astype(jnp.int32)


def tree_lists(key):
    tree_key = jax.random.fold_in(key, 4099)
    fine_numbers = curve_numbers((BX, BY, BZ), N_CURVE)
    coarse_numbers = curve_numbers((BX // 2, BY // 2, BZ // 2), N_CURVE)
    size_x, size_y, size_z = coarse_numbers.shape
    fill_rates = jax.random.randint(jax.random.fold_in(tree_key, 1), (size_x, size_y, size_z), 2, 9)
    fill_rates = fill_rates.at[-4:, -4:, -4:].set(8)
    samples = jax.random.randint(jax.random.fold_in(tree_key, 2), (2 * size_x, 2 * size_y, 2 * size_z), 0, 8)
    spread_rates = jnp.repeat(jnp.repeat(jnp.repeat(fill_rates, 2, 0), 2, 1), 2, 2)
    fine_present = samples < spread_rates
    coarse_present = fine_present.reshape(size_x, 2, size_y, 2, size_z, 2).any(axis=(1, 3, 5))
    fine_count = BX * BY * BZ
    return (level_lists(fine_present, fine_numbers, fine_count), level_lists(coarse_present, coarse_numbers, fine_count // 8))


def draw_fine_lists(key, part):
    return tree_lists(key)[0]


def draw_coarse_lists(key, part):
    return tree_lists(key)[1]


def block_levels(stream_key, dims, pieces, low, top_value):
    gain, own = 1.0, jax.random.fold_in(stream_key, 6)
    for axis_at, shards_of in pieces:
        draws = jnp.exp(jax.random.uniform(jax.random.fold_in(own, axis_at), (shards_of,), jnp.float32, low / len(pieces), top_value / len(pieces)))
        gain = gain * jnp.repeat(draws, dims[axis_at] // shards_of).reshape([-1 if axis == axis_at else 1 for axis in range(len(dims))])
    return gain


def noise(own_key, shape, width, reach, split=(), kind=jnp.bfloat16):
    gain = block_levels(own_key, shape, split, -0.22, 0.18) if split else 1.0
    entries = jax.random.normal(own_key, shape, jnp.float32) * width * gain
    return jnp.minimum(jnp.maximum(entries, -reach), reach).astype(kind)


def setup_inputs(seed: int = 0) -> dict:
    seeds = jax.random.split(jax.random.key(seed), 8)
    return {
        "multipole": noise(seeds[0], (P_SIZE, BOXES), 1.0, 6.0, ((1, 32),)),
        "upward_maps": noise(seeds[1], (8, P_SIZE, P_SIZE), (8 * P_SIZE) ** -0.5, 0.15625),
        "transfer_maps": noise(seeds[2], (OFFS, P_SIZE, P_SIZE), (189 * P_SIZE) ** -0.5, 0.03125),
        "downward_maps": noise(seeds[3], (8, P_SIZE, P_SIZE), P_SIZE ** -0.5, 0.5),
        "check_inverse": noise(seeds[4], (P_SIZE, P_SIZE), P_SIZE ** -0.5, 0.5),
        "fine_lists": draw_fine_lists(jax.random.fold_in(seeds[7], 71), 0),
        "coarse_lists": draw_coarse_lists(jax.random.fold_in(seeds[7], 71), 0),
    }


SHIFTS = [(first_axis, second_axis, third_axis) for first_axis in range(-3, 4) for second_axis in range(-3, 4) for third_axis in range(-3, 4) if max(abs(first_axis), abs(second_axis), abs(third_axis)) >= 2]


def curve_layout(devices):
    levels = devices.bit_length() - 1
    limits = (2 ** (levels // 3), 2 ** ((levels + 1) // 3), 2 ** ((levels + 2) // 3))
    numbers = np.arange(devices)
    places = [np.zeros(devices, np.int64) for axis_number in range(3)]
    for bit_place in range(levels):
        places[2 - bit_place % 3] += ((numbers >> bit_place) & 1) << (bit_place // 3)
    lexical = (places[0] * limits[1] + places[1]) * limits[2] + places[2]
    return np.argsort(lexical), limits


def to_grid(flattened, brick, devices):
    lookup, limits = curve_layout(devices)
    leading = flattened.shape[0]
    bricks = flattened.reshape(leading, devices, brick[0], brick[1], brick[2])[:, lookup]
    bricks = bricks.reshape(leading, limits[0], limits[1], limits[2], brick[0], brick[1], brick[2])
    return bricks.transpose(0, 1, 4, 2, 5, 3, 6).reshape(leading, limits[0] * brick[0], limits[1] * brick[1], limits[2] * brick[2])


def from_grid(numbering, brick, devices):
    lookup, limits = curve_layout(devices)
    leading = numbering.shape[0]
    bricks = numbering.reshape(leading, limits[0], brick[0], limits[1], brick[1], limits[2], brick[2])
    bricks = bricks.transpose(0, 1, 3, 5, 2, 4, 6).reshape(leading, devices, brick[0] * brick[1] * brick[2])
    return bricks[:, np.argsort(lookup)].reshape(leading, -1)


def translate(density, lists, operators):
    channels = density.shape[0]
    extent = density.shape[1:]
    padded = jnp.pad(density.astype(jnp.float32), ((0, 0), (3, 3), (3, 3), (3, 3)))
    running = jnp.zeros(density.shape, jnp.float32)
    for number, offset in enumerate(SHIFTS):
        targets = []
        sources = []
        for axis_number in range(3):
            start_at = 1 if offset[axis_number] == -3 else 0
            stride = 2 if abs(offset[axis_number]) == 3 else 1
            targets.append(slice(start_at, extent[axis_number], stride))
            sources.append(slice(3 + offset[axis_number] + start_at, 3 + offset[axis_number] + extent[axis_number], stride))
        present = (lists[number][targets[0], targets[1], targets[2]] >= 0).astype(jnp.float32)
        picked = padded[:, sources[0], sources[1], sources[2]] * present
        shape_now = picked.shape
        product = jnp.dot(operators[number].astype(jnp.float32), picked.reshape(channels, -1), precision=lax.Precision.HIGHEST)
        running = running.at[:, targets[0], targets[1], targets[2]].add(product.reshape(shape_now))
    return running


def reference(multipole, upward_maps, transfer_maps, downward_maps, check_inverse, fine_lists, coarse_lists):
    channels = multipole.shape[0]
    fine_brick = (BX, BY, BZ)
    coarse_brick = (BX // 2, BY // 2, BZ // 2)
    fine_grid = to_grid(multipole, fine_brick, N_CURVE)
    size_x, size_y, size_z = fine_grid.shape[1:]
    children = fine_grid.reshape(channels, size_x // 2, 2, size_y // 2, 2, size_z // 2, 2).transpose(2, 4, 6, 0, 1, 3, 5).reshape(8, channels, -1)
    parents = jnp.einsum("opq,oqc->pc", upward_maps.astype(jnp.float32), children.astype(jnp.float32), precision=lax.Precision.HIGHEST).astype(jnp.bfloat16)
    parent_grid = parents.reshape(channels, size_x // 2, size_y // 2, size_z // 2)
    coarse_check = 0.5 * translate(parent_grid, to_grid(coarse_lists, coarse_brick, N_CURVE), transfer_maps)
    coarse_local = coarse_check.astype(jnp.bfloat16).reshape(channels, -1)
    spread = jnp.einsum("opq,qc->opc", downward_maps.astype(jnp.float32), coarse_local.astype(jnp.float32), precision=lax.Precision.HIGHEST)
    spread = spread.reshape(2, 2, 2, channels, size_x // 2, size_y // 2, size_z // 2).transpose(3, 4, 0, 5, 1, 6, 2).reshape(channels, size_x, size_y, size_z)
    fine_check = translate(fine_grid, to_grid(fine_lists, fine_brick, N_CURVE), transfer_maps)
    fine_total = (fine_check + spread).astype(jnp.bfloat16)
    result = jnp.dot(check_inverse, fine_total.reshape(channels, -1), preferred_element_type=jnp.float32).astype(jnp.bfloat16)
    return from_grid(result.reshape(channels, size_x, size_y, size_z), fine_brick, N_CURVE)
```

```python
import itertools

import jax
import jax.numpy as jnp
import numpy as np
from jax import lax
from jax.experimental import pallas as pl
from jax.experimental.pallas import tpu as pltpu
from jax.sharding import PartitionSpec as P

BX, BY, BZ = 8, 8, 16
PX, PY, PZ = BX // 2, BY // 2, BZ // 2
LANES = PX * PY * PZ
EXT = (PX, PY, PZ)
BF = jnp.bfloat16
F32 = jnp.float32
SHIFTS = [
    d for d in itertools.product(range(-3, 4), repeat=3) if max(abs(d[0]), abs(d[1]), abs(d[2])) >= 2
]
NUMBER = {d: n for n, d in enumerate(SHIFTS)}
MIB = 1 << 20


def grid_counts(levels):
    return (2 ** (levels // 3), 2 ** ((levels + 1) // 3), 2 ** ((levels + 2) // 3))


def decode(position, levels):
    coords = [0, 0, 0]
    for bit_place in range(levels):
        coords[2 - bit_place % 3] += (position >> bit_place & 1) << (bit_place // 3)
    return coords


def encode(coords, levels):
    number = 0
    for bit_place in range(levels):
        number += (coords[2 - bit_place % 3] >> (bit_place // 3) & 1) << bit_place
    return number


def swap_pairs(devices, levels, axis, odd):
    pairs = []
    for number in range(devices):
        coords = decode(number, levels)
        if coords[axis] % 2 == odd and coords[axis] + 1 < grid_counts(levels)[axis]:
            coords[axis] += 1
            other = encode(coords, levels)
            pairs += [(number, other), (other, number)]
    return pairs


def lane_of(e):
    return (e[0] * PY * PZ + e[1] * PZ + e[2]) % LANES


def coords_of(axis, outside, depth):
    if outside:
        return list(range(-depth, 0)) + list(range(EXT[axis], EXT[axis] + depth))
    return list(range(EXT[axis]))


def elements(kind, depth):
    return itertools.product(*[coords_of(axis, kind[axis], depth) for axis in range(3)])


class Masks:
    def __init__(self):
        self.rows = {}
        self.table = []

    def add(self, name, lanes):
        row = np.zeros(LANES, np.float32)
        row[sorted(lanes)] = 1
        self.rows[name] = len(self.table)
        self.table.append(row)


KINDS_YZ = [(0, 0, 0), (0, 1, 0), (0, 0, 1), (0, 1, 1)]
ALL_KINDS = [tuple(k) for k in itertools.product((0, 1), repeat=3)]


def build_masks():
    masks = Masks()
    every = range(LANES)
    for depth in (1, 2):
        reach = 1 if depth == 1 else 3
        for kind in ALL_KINDS:
            for axis in range(3):
                if kind[axis]:
                    masks.add(
                        ("plus", depth, kind, axis),
                        {lane_of(e) for e in elements(kind, depth) if e[axis] >= EXT[axis]},
                    )
        for axis in range(3):
            kinds = {0: KINDS_YZ, 1: [(0, 0, 0), (0, 0, 1)], 2: [(0, 0, 0)]}[axis]
            for kind in kinds:
                for step in range(-reach, reach + 1):
                    lanes = set()
                    for e in elements(kind, depth):
                        moved = list(e)
                        moved[axis] += step
                        if not 0 <= moved[axis] < EXT[axis]:
                            lanes.add(lane_of(moved))
                    masks.add(("stage", depth, axis, kind, step), lanes)
    for s in range(8):
        masks.add(("zpack", s), {l for l in every if l % PZ == s})
    row = PY * PZ
    low_z = {lane_of((i, 0, k)) for i in range(PX) for k in (-1, PZ)}
    up_z = {lane_of((i, PY - 1, k)) for i in range(PX) for k in (-1, PZ)}
    masks.add(("ysrc", 0), low_z)
    masks.add(("ysrc", 1), up_z)
    for t in range(3):
        masks.add(("ypack", t), {l for l in every if (l % row) // 10 == t})
    masks.add(("xsrc_a", 0), set(range(row)))
    masks.add(("xsrc_a", 1), set(range(LANES - row, LANES)))
    for side, i in ((0, 0), (1, PX - 1)):
        masks.add(("xsrc_b", side), {lane_of((i, j, k)) for j in range(PY) for k in (-1, PZ)})
    for t in range(2):
        masks.add(("xpack_a", t), {l for l in every if l // 64 == t})
    for t in range(8):
        u, v = t % 4, t // 4
        masks.add(("xpack_b", t), {l for l in every if l // 64 == v and l % 8 in (2 * u, 2 * u + 1)})
    return masks


MASKS = build_masks()
TABLE = np.stack(MASKS.table)


def pick(tab, name, yes, no):
    n = MASKS.rows[name]
    row = jnp.broadcast_to(tab[n : n + 1, :], yes.shape).astype(BF)
    return jnp.where(row > 0, yes, no)


def roll(x, by):
    by = by % LANES
    return x if by == 0 else pltpu.roll(x, by, 1)


def padded(x, rows):
    return jnp.concatenate([x, jnp.zeros((rows - x.shape[0], x.shape[1]), x.dtype)], 0)


def octant_order():
    row = np.arange(PX * BY * BZ)
    i, y, z = row // (BY * BZ), row // BZ % BY, row % BZ
    column = (2 * (y % 2) + z % 2) * LANES + i * PY * PZ + (y // 2) * PZ + z // 2
    hot = np.zeros((len(row), len(row)), np.float32)
    hot[row, column] = 1
    return hot


def to_octants(x, hot):
    layer = BY * BZ
    halves = []
    for a in range(2):
        chunk = jnp.concatenate(
            [x[:, (2 * i + a) * layer : (2 * i + a + 1) * layer] for i in range(PX)], 1
        )
        halves.append(jnp.dot(chunk, hot, preferred_element_type=F32))
    return halves


def prep_kernel(par, mult, up, hot, tab, own, coarse, send_a, send_b):
    chans = mult.shape[0]
    rows = own.shape[1]
    halves = to_octants(mult[...], hot[...])
    total = jnp.zeros((chans, LANES), F32)
    pack = [None, None]
    for s in range(8):
        x = halves[s // 4][:, (s % 4) * LANES : (s % 4 + 1) * LANES].astype(BF)
        total = total + jnp.dot(up[s], x, preferred_element_type=F32)
        x = padded(x, rows)
        own[s] = x
        for side in range(2):
            moved = roll(x, s - (PZ - 1) * side)
            pack[side] = moved if s == 0 else pick(tab, ("zpack", s), moved, pack[side])
    c = padded(total.astype(BF), rows)
    coarse[...] = c
    even = par[2] == 0
    send_a[0] = jnp.where(even, pack[1], pack[0])
    send_b[0] = jnp.where(even, pack[0], pack[1])
    send_a[1] = c
    send_b[1] = c


def sides(par, axis, got_a, got_b):
    even = par[axis] == 0
    plus = jnp.where(even, got_a, got_b)
    minus = jnp.where(even, got_b, got_a)
    return plus, minus


def y_kernel(par, own, coarse, got_a, got_b, tab, hz, cz, send_a, send_b):
    p, m = sides(par, 2, got_a[0], got_b[0])
    for s in range(8):
        hz[s] = pick(
            tab, ("plus", 1, (0, 0, 1), 2), roll(p, PZ - s), roll(m, -1 - s)
        )
    p, m = sides(par, 2, got_a[1], got_b[1])
    far = pick(tab, ("plus", 2, (0, 0, 1), 2), roll(p, PZ), roll(m, -PZ))
    cz[...] = far
    even = par[1] == 0
    pack = [[None] * 3, [None] * 3]
    for s in range(8):
        block, t = s // 3, s % 3
        for side in range(2):
            src = pick(tab, ("ysrc", side), hz[s], own[s])
            moved = roll(src, 1 + 10 * t - (PY - 1) * PZ * side)
            pack[side][block] = (
                moved if t == 0 else pick(tab, ("ypack", t), moved, pack[side][block])
            )
    for block in range(3):
        send_a[block] = jnp.where(even, pack[1][block], pack[0][block])
        send_b[block] = jnp.where(even, pack[0][block], pack[1][block])
    for send in (send_a, send_b):
        send[3] = coarse[...]
        send[4] = far


def x_kernel(par, own, coarse, hz, cz, got_a, got_b, tab, hy, hyz, cy, cyz, send_a, send_b):
    row = PY * PZ
    for s in range(8):
        block, t = s // 3, s % 3
        p, m = sides(par, 1, got_a[block], got_b[block])
        p = roll(p, row - 1 - 10 * t)
        m = roll(m, -PZ - 1 - 10 * t)
        hy[s] = pick(tab, ("plus", 1, (0, 1, 0), 1), p, m)
        hyz[s] = pick(tab, ("plus", 1, (0, 1, 1), 1), p, m)
    near = []
    for n, kind in ((3, (0, 1, 0)), (4, (0, 1, 1))):
        p, m = sides(par, 1, got_a[n], got_b[n])
        near.append(pick(tab, ("plus", 2, kind, 1), roll(p, row), roll(m, -row)))
    cy[...] = near[0]
    cyz[...] = near[1]
    even = par[0] == 0
    pack_a = [[None] * 4, [None] * 4]
    pack_b = [None, None]
    for s in range(8):
        block, t = s // 2, s % 2
        u, v = s % 4, s // 4
        for side in range(2):
            a = pick(tab, ("xsrc_a", side), own[s], hy[s])
            b = pick(tab, ("xsrc_b", side), hz[s], hyz[s])
            a = roll(a, 8 + 64 * t - (PX - 1) * row * side)
            b = roll(b, 9 + 2 * u + 64 * v - (PX - 1) * row * side)
            pack_a[side][block] = a if t == 0 else pick(tab, ("xpack_a", t), a, pack_a[side][block])
            pack_b[side] = b if s == 0 else pick(tab, ("xpack_b", s), b, pack_b[side])
    for block in range(4):
        send_a[block] = jnp.where(even, pack_a[1][block], pack_a[0][block])
        send_b[block] = jnp.where(even, pack_a[0][block], pack_a[1][block])
    send_a[4] = jnp.where(even, pack_b[1], pack_b[0])
    send_b[4] = jnp.where(even, pack_b[0], pack_b[1])
    for send in (send_a, send_b):
        send[5] = coarse[...]
        send[6] = near[0]
        send[7] = cz[...]
        send[8] = near[1]


def offset_sets():
    fours = []

    def add(offsets):
        start = len(fours)
        for n in range(0, len(offsets), 4):
            fours.append(tuple(offsets[n : n + 4]))
        return list(range(start, len(fours)))

    small = range(-2, 3)
    sets = {}
    sets["free"] = add([d for d in SHIFTS if max(map(abs, d)) == 2])
    for axis in range(3):
        for sign in (-3, 3):
            sets[axis, sign] = add(
                [d for d in SHIFTS if d[axis] == sign and all(abs(d[o]) <= 2 for o in range(3) if o != axis)]
            )
    for sx in (-3, 3):
        for sy in (-3, 3):
            sets["xy", sx, sy] = add([(sx, sy, z) for z in small])
        for sz in (-3, 3):
            sets["xz", sx, sz] = add([(sx, y, sz) for y in small])
    for sy in (-3, 3):
        for sz in (-3, 3):
            sets["yz", sy, sz] = add([(x, sy, sz) for x in range(-3, 4)])
    return fours, sets


FOURS, SETS = offset_sets()
SIGN = (3, -3)


def jobs_of(j):
    one, two = j // 2, j % 2
    big = SETS["free"] + SETS[0, SIGN[one]] + SETS[1, SIGN[two]] + SETS["xy", SIGN[one], SIGN[two]]
    mid = SETS[2, SIGN[two]] + SETS["xz", SIGN[one], SIGN[two]]
    small = SETS["yz", SIGN[one], SIGN[two]]
    return [
        (big, (one, two, 0), (one, two, 1)),
        (mid, (one, 0, two), (one, 1, two)),
        (small, (0, one, two), (1, one, two)),
    ]


def slot_of(octant, d):
    place = [octant[n] + d[n] for n in range(3)]
    moved = [min(max(p // 2, -1), 1) for p in place]
    s = [p % 2 for p in place]
    return ((moved[0] + 1) * 9 + (moved[1] + 1) * 3 + moved[2] + 1) * 8 + 4 * s[0] + 2 * s[1] + s[2]


def octant_number(o):
    return 4 * o[0] + 2 * o[1] + o[2]


def fine_table():
    rows, shape = [], None
    for j in range(4):
        row, form = [], []
        for fours, first, second in jobs_of(j):
            row += [octant_number(first), octant_number(second)]
            counts = []
            for f in fours:
                row.append(f)
                counts.append(len(FOURS[f]))
                for d in FOURS[f]:
                    row += [NUMBER[d], slot_of(first, d), slot_of(second, d)]
            form.append(counts)
        assert shape is None or shape == form
        rows.append(row)
        shape = form
    return np.array(rows, np.int32), shape


FINE_TABLE, FINE_FORM = fine_table()


def coarse_table(spare):
    rows = []
    for four in FOURS:
        for n in range(4):
            d = four[n] if n < len(four) else None
            if d is None:
                rows.append((0, spare, 3 * 7 + 3, 0))
            else:
                rows.append((NUMBER[d], NUMBER[d], (d[0] + 3) * 7 + d[1] + 3, d[2] + 3))
    return np.array(rows, np.int32)


def rest_order(offsets):
    hot = np.zeros((offsets, 4 * LANES), np.float32)
    for n, four in enumerate(FOURS):
        for place, d in enumerate(four):
            hot[NUMBER[d], place * LANES + n] = 1
    return hot


def operator_kernel(w, order, main, rest):
    block, chans, offsets = w.shape
    at = pl.multiple_of(pl.program_id(0) * block, block)
    main[:, pl.ds(at, block), :] = jnp.transpose(w[:, 0:LANES, :], (2, 0, 1))
    left = chans - LANES
    stacked = []
    for n in range(block):
        y = jnp.dot(w[n, LANES:chans, :], order[...], preferred_element_type=F32).astype(BF)
        y = padded(y, 32)
        stacked.append(
            jnp.concatenate([y[:, m * LANES : (m + 1) * LANES] for m in range(4)], 0)
        )
    turned = jnp.transpose(jnp.stack(stacked), (2, 0, 1))
    rest[:, pl.ds(at, block), :] = turned[0 : rest.shape[0]]


def mask_kernel(fine, hot, out):
    keep = (fine[...] >= 0).astype(F32).astype(BF)
    halves = to_octants(keep, hot[...])
    offsets = fine.shape[0]
    for s in range(8):
        out[s, 0:offsets, :] = halves[s // 4][:, (s % 4) * LANES : (s % 4 + 1) * LANES]


def shifted(tab, depth, axis, kind, step, inside, outside):
    if step == 0:
        return inside
    stride = (PY * PZ, PZ, 1)[axis]
    return roll(pick(tab, ("stage", depth, axis, kind, step), outside, inside), -step * stride)


def dot_pieces(pieces):
    left = jnp.concatenate([p[0] for p in pieces], 1)
    right = jnp.concatenate([p[1] for p in pieces], 0)
    return jnp.dot(left, right, preferred_element_type=F32)


def main_kernel(
    par, ft, ct, own, hz, hy, hyz, coarse, cz, cy, cyz, got_a, got_b, tab, main, rest, keep, clist,
    down, inverse, hot, out, slots, acc, cacc, plane, cmask,
):
    chans = acc.shape[1]
    rows = own.shape[1]
    row = PY * PZ
    for s in range(8):
        block, t = s // 2, s % 2
        u, v = s % 4, s // 4
        p, m = sides(par, 0, got_a[block], got_b[block])
        p, m = roll(p, -8 - 64 * t), roll(m, -8 - 64 * t + (PX - 1) * row)
        hx = pick(tab, ("plus", 1, (1, 0, 0), 0), p, m)
        hxy = pick(tab, ("plus", 1, (1, 1, 0), 0), p, m)
        p, m = sides(par, 0, got_a[4], got_b[4])
        p, m = roll(p, -9 - 2 * u - 64 * v), roll(m, -9 - 2 * u - 64 * v + (PX - 1) * row)
        hxz = pick(tab, ("plus", 1, (1, 0, 1), 0), p, m)
        hxyz = pick(tab, ("plus", 1, (1, 1, 1), 0), p, m)
        inner = {(0, 0, 0): own[s], (0, 1, 0): hy[s], (0, 0, 1): hz[s], (0, 1, 1): hyz[s]}
        outer = {(0, 0, 0): hx, (0, 1, 0): hxy, (0, 0, 1): hxz, (0, 1, 1): hxyz}
        for dx in (-1, 0, 1):
            x = {k: shifted(tab, 1, 0, k, dx, inner[k], outer[k]) for k in KINDS_YZ}
            for dy in (-1, 0, 1):
                y = {
                    z: shifted(tab, 1, 1, (0, 0, z), dy, x[0, 0, z], x[0, 1, z]) for z in (0, 1)
                }
                for dz in (-1, 0, 1):
                    n = ((dx + 1) * 9 + (dy + 1) * 3 + dz + 1) * 8 + s
                    slots[n] = shifted(tab, 1, 2, (0, 0, 0), dz, y[0], y[1])
    inner = {(0, 0, 0): coarse[...], (0, 1, 0): cy[...], (0, 0, 1): cz[...], (0, 1, 1): cyz[...]}
    outer = {}
    for n, k in ((5, (0, 0, 0)), (6, (0, 1, 0)), (7, (0, 0, 1)), (8, (0, 1, 1))):
        p, m = sides(par, 0, got_a[n], got_b[n])
        outer[k] = pick(tab, ("plus", 2, (1, k[1], k[2]), 0), p, m)
    for dx in range(-3, 4):
        x = {k: shifted(tab, 2, 0, k, dx, inner[k], outer[k]) for k in KINDS_YZ}
        for dy in range(-3, 4):
            for z in (0, 1):
                plane[((dx + 3) * 7 + dy + 3) * 2 + z] = shifted(
                    tab, 2, 1, (0, 0, z), dy, x[0, 0, z], x[0, 1, z]
                )
    offsets = clist.shape[0]
    cmask[...] = jnp.zeros_like(cmask)
    cmask[0:offsets, :] = (clist[...] >= 0).astype(F32)
    acc[...] = jnp.zeros_like(acc)
    cacc[...] = jnp.zeros_like(cacc)
    first = MASKS.rows["stage", 2, 2, (0, 0, 0), -3]

    def coarse_body(it, carry):
        pieces = []
        for f in range(7):
            rests = []
            four = it * 7 + f
            for n in range(4):
                at = (four * 4 + n) * 4
                d, md, pn, dz = ct[at], ct[at + 1], ct[at + 2], ct[at + 3]
                far = jnp.broadcast_to(tab[pl.ds(first + dz, 1), :], (rows, LANES)).astype(BF)
                src = jnp.where(far > 0, plane[pn * 2 + 1], plane[pn * 2])
                src = pltpu.roll(src, LANES + 3 - dz, 1)
                mask = jnp.broadcast_to(cmask[pl.ds(md, 1), :], (rows, LANES)).astype(BF)
                x = src * mask
                pieces.append((main[d], x[0:LANES]))
                rests.append(x[LANES:rows])
            pieces.append((rest[four], jnp.concatenate(rests, 0)))
        cacc[...] += dot_pieces(pieces)
        return carry

    lax.fori_loop(0, len(FOURS) // 7, coarse_body, 0)

    def fine_body(j, carry):
        at = j * FINE_TABLE.shape[1]
        for counts in FINE_FORM:
            first_o, second_o = ft[at], ft[at + 1]
            at = at + 2
            pieces = []

            def flush(part):
                got = dot_pieces(part)
                acc[first_o] += got[:, 0:LANES]
                acc[second_o] += got[:, LANES:]

            for count in counts:
                four = ft[at]
                at = at + 1
                rests = []
                for n in range(count):
                    d, one, two = ft[at], ft[at + 1], ft[at + 2]
                    at = at + 3
                    x = []
                    for slot, o in ((one, first_o), (two, second_o)):
                        mask = jnp.broadcast_to(keep[o, pl.ds(d, 1), :], (rows, LANES)).astype(BF)
                        x.append(slots[slot] * mask)
                    x = jnp.concatenate(x, 1)
                    pieces.append((main[d], x[0:LANES]))
                    rests.append(x[LANES:rows])
                if count < 4:
                    rests.append(jnp.zeros((32 * (4 - count), 2 * LANES), BF))
                pieces.append((rest[four], jnp.concatenate(rests, 0)))
                while len(pieces) >= 20:
                    flush(pieces[:20])
                    pieces = pieces[20:]
            if pieces:
                flush(pieces)
        return carry

    lax.fori_loop(0, 4, fine_body, 0)
    local = (0.5 * cacc[...]).astype(BF)
    total = []
    for s in range(8):
        spread = jnp.dot(down[s], local, preferred_element_type=F32)
        total.append((acc[s] + spread).astype(BF))
    density = jnp.dot(inverse[...], jnp.concatenate(total, 1), preferred_element_type=F32).astype(BF)
    half = 4 * LANES
    layer = BY * BZ
    for a in range(2):
        natural = lax.dot_general(
            density[:, a * half : (a + 1) * half],
            hot[...],
            (((1,), (1,)), ((), ())),
            preferred_element_type=F32,
        ).astype(BF)
        for i in range(PX):
            out[:, (2 * i + a) * layer : (2 * i + a + 1) * layer] = natural[:, i * layer : (i + 1) * layer]


VMEM = pl.BlockSpec(memory_space=pltpu.VMEM)
SMEM = pl.BlockSpec(memory_space=pltpu.SMEM)


def call(kernel, name, smem, operands, outs, limit, scratch=(), flops=0, bytes_=0):
    shapes = [jax.ShapeDtypeStruct(s, t) for s, t in outs]
    return pl.pallas_call(
        kernel,
        name=name,
        in_specs=[SMEM] * smem + [VMEM] * (len(operands) - smem),
        out_specs=[VMEM] * len(shapes),
        out_shape=shapes,
        scratch_shapes=list(scratch),
        compiler_params=pltpu.CompilerParams(vmem_limit_bytes=limit),
        cost_estimate=pl.CostEstimate(flops=flops, bytes_accessed=bytes_, transcendentals=0),
    )(*operands)


def local(
    multipole, upward_maps, transfer_maps, downward_maps, check_inverse, fine_lists, coarse_lists
):
    chans = multipole.shape[0]
    offsets = transfer_maps.shape[0]
    rows = (chans + 31) // 32 * 32
    devices = lax.axis_size("curve")
    levels = devices.bit_length() - 1
    limits = grid_counts(levels)
    position = lax.axis_index("curve")
    par = jnp.stack([position >> (2 - axis) & 1 for axis in range(3)]).astype(jnp.int32)
    hot = jnp.asarray(octant_order(), BF)
    tab = jnp.asarray(TABLE)
    row_pad = (offsets + 8) // 8 * 8

    def exchange(axis, a, b):
        got_a = lax.ppermute(a, "curve", swap_pairs(devices, levels, axis, 0))
        pairs = swap_pairs(devices, levels, axis, 1)
        got_b = lax.ppermute(b, "curve", pairs) if pairs else jnp.zeros_like(b)
        return got_a, got_b

    full = ((8, rows, LANES), BF)
    one = ((rows, LANES), BF)
    own, coarse, a, b = call(
        prep_kernel, "prep", 1, (par, multipole, upward_maps, hot, tab),
        [full, one, ((2, rows, LANES), BF), ((2, rows, LANES), BF)], 16 * MIB,
        flops=10**9, bytes_=2 * MIB,
    )
    za, zb = exchange(2, a, b)
    hz, cz, a, b = call(
        y_kernel, "pack_y", 1, (par, own, coarse, za, zb, tab),
        [full, one, ((5, rows, LANES), BF), ((5, rows, LANES), BF)], 16 * MIB,
        flops=10**6, bytes_=2 * MIB,
    )
    ya, yb = exchange(1, a, b)
    hy, hyz, cy, cyz, a, b = call(
        x_kernel, "pack_x", 1, (par, own, coarse, hz, cz, ya, yb, tab),
        [full, full, one, one, ((9, rows, LANES), BF), ((9, rows, LANES), BF)], 16 * MIB,
        flops=10**6, bytes_=2 * MIB,
    )
    xa, xb = exchange(0, a, b)

    block = 8
    rests = (len(FOURS) + 7) // 8 * 8
    turned = jnp.transpose(transfer_maps, (1, 2, 0))
    order = jnp.asarray(rest_order(offsets), BF)
    main, rest = pl.pallas_call(
        operator_kernel,
        name="operators",
        grid=(chans // block,),
        in_specs=[
            pl.BlockSpec((block, chans, offsets), lambda n: (n, 0, 0)),
            pl.BlockSpec(order.shape, lambda n: (0, 0)),
        ],
        out_specs=[VMEM, VMEM],
        out_shape=[
            jax.ShapeDtypeStruct((offsets, chans, LANES), BF),
            jax.ShapeDtypeStruct((rests, chans, LANES), BF),
        ],
        compiler_params=pltpu.CompilerParams(vmem_limit_bytes=30 * MIB),
        cost_estimate=pl.CostEstimate(flops=10**10, bytes_accessed=18 * MIB, transcendentals=0),
    )(turned, order)
    (keep,) = call(
        mask_kernel, "masks", 0, (fine_lists, hot), [((8, row_pad, LANES), F32)], 16 * MIB,
        flops=10**9, bytes_=2 * MIB,
    )
    ft = jnp.asarray(FINE_TABLE.reshape(-1))
    ct = jnp.asarray(coarse_table(row_pad - 1).reshape(-1))
    (out,) = call(
        main_kernel, "translate", 3,
        (par, ft, ct, own, hz, hy, hyz, coarse, cz, cy, cyz, xa, xb, tab, main, rest, keep,
         coarse_lists, downward_maps, check_inverse, hot),
        [((chans, multipole.shape[1]), BF)],
        44 * MIB,
        scratch=[
            pltpu.VMEM((216, rows, LANES), BF),
            pltpu.VMEM((8, chans, LANES), F32),
            pltpu.VMEM((chans, LANES), F32),
            pltpu.VMEM((98, rows, LANES), BF),
            pltpu.VMEM((row_pad, LANES), F32),
        ],
        flops=2 * 10**10, bytes_=20 * MIB,
    )
    return out


def solution(mesh):
    placed = (P(None, "curve"), P(), P(), P(), P(), P(None, "curve"), P(None, "curve"))
    return jax.shard_map(
        local, mesh=mesh, in_specs=placed, out_specs=P(None, "curve"), check_vma=False
    )
```

```python
import functools
import itertools

import jax
import jax.numpy as jnp
import numpy as np
from jax import lax
from jax.experimental import pallas as pl
from jax.experimental.pallas import tpu as pltpu
from jax.sharding import PartitionSpec as P

BX, BY, BZ = 8, 8, 16
PX, PY, PZ = BX // 2, BY // 2, BZ // 2
LANES = PX * PY * PZ
EXT = (PX, PY, PZ)
BF = jnp.bfloat16
F32 = jnp.float32
SHIFTS = [
    d for d in itertools.product(range(-3, 4), repeat=3) if max(abs(d[0]), abs(d[1]), abs(d[2])) >= 2
]
NUMBER = {d: n for n, d in enumerate(SHIFTS)}
MIB = 1 << 20


def grid_counts(levels):
    return (2 ** (levels // 3), 2 ** ((levels + 1) // 3), 2 ** ((levels + 2) // 3))


def decode(position, levels):
    coords = [0, 0, 0]
    for bit_place in range(levels):
        coords[2 - bit_place % 3] += (position >> bit_place & 1) << (bit_place // 3)
    return coords


def encode(coords, levels):
    number = 0
    for bit_place in range(levels):
        number += (coords[2 - bit_place % 3] >> (bit_place // 3) & 1) << bit_place
    return number


def swap_pairs(devices, levels, axis, odd):
    pairs = []
    for number in range(devices):
        coords = decode(number, levels)
        if coords[axis] % 2 == odd and coords[axis] + 1 < grid_counts(levels)[axis]:
            coords[axis] += 1
            other = encode(coords, levels)
            pairs += [(number, other), (other, number)]
    return pairs


def lane_of(e):
    return (e[0] * PY * PZ + e[1] * PZ + e[2]) % LANES


def coords_of(axis, outside, depth):
    if outside:
        return list(range(-depth, 0)) + list(range(EXT[axis], EXT[axis] + depth))
    return list(range(EXT[axis]))


def elements(kind, depth):
    return itertools.product(*[coords_of(axis, kind[axis], depth) for axis in range(3)])


class Masks:
    def __init__(self):
        self.rows = {}
        self.table = []

    def add(self, name, lanes):
        row = np.zeros(LANES, np.float32)
        row[sorted(lanes)] = 1
        self.rows[name] = len(self.table)
        self.table.append(row)


KINDS_YZ = [(0, 0, 0), (0, 1, 0), (0, 0, 1), (0, 1, 1)]
ALL_KINDS = [tuple(k) for k in itertools.product((0, 1), repeat=3)]


def build_masks():
    masks = Masks()
    every = range(LANES)
    for depth in (1, 2):
        reach = 1 if depth == 1 else 3
        for kind in ALL_KINDS:
            for axis in range(3):
                if kind[axis]:
                    masks.add(
                        ("plus", depth, kind, axis),
                        {lane_of(e) for e in elements(kind, depth) if e[axis] >= EXT[axis]},
                    )
        for axis in range(3):
            kinds = {0: KINDS_YZ, 1: [(0, 0, 0), (0, 0, 1)], 2: [(0, 0, 0)]}[axis]
            for kind in kinds:
                for step in range(-reach, reach + 1):
                    lanes = set()
                    for e in elements(kind, depth):
                        moved = list(e)
                        moved[axis] += step
                        if not 0 <= moved[axis] < EXT[axis]:
                            lanes.add(lane_of(moved))
                    masks.add(("stage", depth, axis, kind, step), lanes)
    for d in itertools.product((-1, 0, 1), repeat=3):
        for axis in range(3):
            lanes = set()
            for e in itertools.product(*map(range, EXT)):
                moved = [e[n] + d[n] for n in range(3)]
                if not 0 <= moved[axis] < EXT[axis]:
                    lanes.add(lane_of(moved))
            if d[axis]:
                masks.add(("out", d, axis), lanes)
    for s in range(8):
        masks.add(("zpack", s), {l for l in every if l % PZ == s})
    row = PY * PZ
    low_z = {lane_of((i, 0, k)) for i in range(PX) for k in (-1, PZ)}
    up_z = {lane_of((i, PY - 1, k)) for i in range(PX) for k in (-1, PZ)}
    masks.add(("ysrc", 0), low_z)
    masks.add(("ysrc", 1), up_z)
    for t in range(3):
        masks.add(("ypack", t), {l for l in every if (l % row) // 10 == t})
    masks.add(("xsrc_a", 0), set(range(row)))
    masks.add(("xsrc_a", 1), set(range(LANES - row, LANES)))
    for side, i in ((0, 0), (1, PX - 1)):
        masks.add(("xsrc_b", side), {lane_of((i, j, k)) for j in range(PY) for k in (-1, PZ)})
    for side, i in ((0, (0, 1)), (1, (PX - 2, PX - 1))):
        masks.add(
            ("cy", side),
            {lane_of((n, j, k)) for n in i for j in (-2, -1, PY, PY + 1) for k in range(PZ)},
        )
    masks.add("half", {l for l in every if l < LANES // 2})
    masks.add("mid", {l for l in every if 2 <= l % PZ < 6})
    for t in range(2):
        masks.add(("xpack_a", t), {l for l in every if l // 64 == t})
    for t in range(8):
        u, v = t % 4, t // 4
        masks.add(("xpack_b", t), {l for l in every if l // 64 == v and l % 8 in (2 * u, 2 * u + 1)})
    return masks


MASKS = build_masks()
TABLE = np.stack(MASKS.table)


def pick(tab, name, yes, no):
    n = MASKS.rows[name]
    row = jnp.broadcast_to(tab[n : n + 1, :], yes.shape).astype(BF)
    return jnp.where(row > 0, yes, no)


def pick_row(tab, n, yes, no):
    row = jnp.broadcast_to(tab[pl.ds(n, 1), :], yes.shape).astype(BF)
    return jnp.where(row > 0, yes, no)


def turn_by(x, by):
    return pltpu.roll(x, lax.rem(by + 4 * LANES, LANES), 1)


def roll(x, by):
    by = by % LANES
    return x if by == 0 else pltpu.roll(x, by, 1)


def padded(x, rows):
    return jnp.concatenate([x, jnp.zeros((rows - x.shape[0], x.shape[1]), x.dtype)], 0)


def octant_order():
    row = np.arange(PX * BY * BZ)
    i, y, z = row // (BY * BZ), row // BZ % BY, row % BZ
    column = (2 * (y % 2) + z % 2) * LANES + i * PY * PZ + (y // 2) * PZ + z // 2
    hot = np.zeros((len(row), len(row)), np.float32)
    hot[row, column] = 1
    return hot


def to_octants(x, hot):
    layer = BY * BZ
    halves = []
    for a in range(2):
        chunk = jnp.concatenate(
            [x[:, (2 * i + a) * layer : (2 * i + a + 1) * layer] for i in range(PX)], 1
        )
        halves.append(jnp.dot(chunk, hot, preferred_element_type=F32))
    return halves


def prep_kernel(
    par, mult_hbm, up_hbm, hot_hbm, tab_hbm, own, coarse, send_a, send_b, mult, up, hot, tab, sems
):
    copies = [
        pltpu.make_async_copy(src, dst, sems.at[n])
        for n, (src, dst) in enumerate(
            ((mult_hbm, mult), (hot_hbm, hot), (up_hbm, up), (tab_hbm, tab))
        )
    ]
    for copy in copies:
        copy.start()
    chans = mult.shape[0]
    rows = own.shape[1]
    copies[0].wait()
    copies[1].wait()
    halves = to_octants(mult[...], hot[...])
    copies[2].wait()
    copies[3].wait()
    total = jnp.zeros((chans, LANES), F32)
    pack = [None, None]
    for s in range(8):
        x = halves[s // 4][:, (s % 4) * LANES : (s % 4 + 1) * LANES].astype(BF)
        total = total + jnp.dot(up[s], x, preferred_element_type=F32)
        x = padded(x, rows)
        own[s] = x
        for side in range(2):
            moved = roll(x, s - (PZ - 1) * side)
            pack[side] = moved if s == 0 else pick(tab, ("zpack", s), moved, pack[side])
    c = padded(total.astype(BF), rows)
    coarse[...] = c
    even = par[2] == 0
    send_a[0] = jnp.where(even, pack[1], pack[0])
    send_b[0] = jnp.where(even, pack[0], pack[1])
    send_a[1] = c
    send_b[1] = c


def sides(par, axis, got_a, got_b):
    even = par[axis] == 0
    plus = jnp.where(even, got_a, got_b)
    minus = jnp.where(even, got_b, got_a)
    return plus, minus


def y_kernel(par, own, coarse, got_a, got_b, tab, hz, cz, send_a, send_b):
    p, m = sides(par, 2, got_a[0], got_b[0])
    for s in range(8):
        hz[s] = pick(
            tab, ("plus", 1, (0, 0, 1), 2), roll(p, PZ - s), roll(m, -1 - s)
        )
    p, m = sides(par, 2, got_a[1], got_b[1])
    far = pick(tab, ("plus", 2, (0, 0, 1), 2), roll(p, PZ), roll(m, -PZ))
    cz[...] = far
    even = par[1] == 0
    pack = [[None] * 3, [None] * 3]
    for s in range(8):
        block, t = s // 3, s % 3
        for side in range(2):
            src = pick(tab, ("ysrc", side), hz[s], own[s])
            moved = roll(src, 1 + 10 * t - (PY - 1) * PZ * side)
            pack[side][block] = (
                moved if t == 0 else pick(tab, ("ypack", t), moved, pack[side][block])
            )
    for block in range(3):
        send_a[block] = jnp.where(even, pack[1][block], pack[0][block])
        send_b[block] = jnp.where(even, pack[0][block], pack[1][block])
    for send in (send_a, send_b):
        send[3] = coarse[...]
        send[4] = far


def x_kernel(par, own, coarse, hz, cz, got_a, got_b, tab, hy, hyz, cy, cyz, *sends):
    row = PY * PZ
    for s in range(8):
        block, t = s // 3, s % 3
        p, m = sides(par, 1, got_a[block], got_b[block])
        p = roll(p, row - 1 - 10 * t)
        m = roll(m, -PZ - 1 - 10 * t)
        hy[s] = pick(tab, ("plus", 1, (0, 1, 0), 1), p, m)
        hyz[s] = pick(tab, ("plus", 1, (0, 1, 1), 1), p, m)
    near = []
    for n, kind in ((3, (0, 1, 0)), (4, (0, 1, 1))):
        p, m = sides(par, 1, got_a[n], got_b[n])
        near.append(pick(tab, ("plus", 2, kind, 1), roll(p, row), roll(m, -row)))
    cy[...] = near[0]
    cyz[...] = near[1]
    half = LANES // 2
    other = roll(near[0], half)
    low = pick(tab, "half", coarse[...], pick(tab, ("cy", 0), near[0], other))
    high = pick(tab, "half", pick(tab, ("cy", 1), near[0], other), coarse[...])
    edges = pick(tab, "mid", roll(near[1], 4), cz[...])
    for send, odd in zip(sends, (0, 1)):
        side = par[0] if odd else 1 - par[0]
        far = (PX - 1) * row * side
        whole, line = [None] * 4, None
        for s in range(8):
            block, t = s // 2, s % 2
            u, v = s % 4, s // 4
            a = pick_row(tab, MASKS.rows["xsrc_a", 0] + side, own[s], hy[s])
            b = pick_row(tab, MASKS.rows["xsrc_b", 0] + side, hz[s], hyz[s])
            a = turn_by(a, 8 + 64 * t - far)
            b = turn_by(b, 9 + 2 * u + 64 * v - far)
            whole[block] = a if t == 0 else pick(tab, ("xpack_a", t), a, whole[block])
            line = b if s == 0 else pick(tab, ("xpack_b", s), b, line)
        for block in range(4):
            send[block] = whole[block]
        send[4] = line
        send[5] = jnp.where(side == 1, high, low)
        send[6] = edges


def planes(tab, kinds, far, plane):
    for dy in range(-3, 4):
        y = {
            z: shifted(tab, 2, 1, (0, 0, z), dy, kinds[far, 0, z], kinds[far, 1, z])
            for z in (0, 1)
        }
        for dz in range(-3, 4):
            plane[(dy + 3) * 7 + dz + 3, :, far * LANES : (far + 1) * LANES] = shifted(
                tab, 2, 2, (0, 0, 0), dz, y[0], y[1]
            )


def put_slots(tab, s, kinds, slots, steps):
    for d in steps:
        n = ((d[0] + 1) * 9 + (d[1] + 1) * 3 + d[2] + 1) * 8 + s
        by = d[0] * PY * PZ + d[1] * PZ + d[2]
        slots[n] = roll(gathered(tab, d, kinds, ()), -by)


def early_kernel(own, hz, hy, hyz, coarse, cz, cy, cyz, tab, slots, plane):
    kinds = {(0, 0, 0): coarse[...], (0, 1, 0): cy[...], (0, 0, 1): cz[...], (0, 1, 1): cyz[...]}
    planes(tab, kinds, 0, plane)
    steps = [(0, dy, dz) for dy in (-1, 0, 1) for dz in (-1, 0, 1) if dy or dz]

    def body(s, carry):
        kinds = {(0, 0, 0): own[s], (0, 1, 0): hy[s], (0, 0, 1): hz[s], (0, 1, 1): hyz[s]}
        put_slots(tab, s, kinds, slots, steps)
        return carry

    lax.fori_loop(0, 8, body, 0)


def offset_sets():
    fours = []

    def add(offsets):
        start = len(fours)
        for turn in range(PX):
            like = [d for d in offsets if d[0] % PX == turn]
            for n in range(0, len(like), 4):
                fours.append(tuple(like[n : n + 4]))
        return list(range(start, len(fours)))

    small = range(-2, 3)
    sets = {}
    sets["free"] = add([d for d in SHIFTS if max(map(abs, d)) == 2])
    for axis in range(3):
        for sign in (-3, 3):
            sets[axis, sign] = add(
                [d for d in SHIFTS if d[axis] == sign and all(abs(d[o]) <= 2 for o in range(3) if o != axis)]
            )
    for sx in (-3, 3):
        for sy in (-3, 3):
            sets["xy", sx, sy] = add([(sx, sy, z) for z in small])
        for sz in (-3, 3):
            sets["xz", sx, sz] = add([(sx, y, sz) for y in small])
    for sy in (-3, 3):
        for sz in (-3, 3):
            sets["yz", sy, sz] = add([(x, sy, sz) for x in range(-3, 4)])
    return fours, sets


FOURS, SETS = offset_sets()
SIGN = (3, -3)


def jobs_of(j):
    one, two = j // 2, j % 2
    big = SETS["free"] + SETS[0, SIGN[one]] + SETS[1, SIGN[two]] + SETS["xy", SIGN[one], SIGN[two]]
    mid = SETS[2, SIGN[two]] + SETS["xz", SIGN[one], SIGN[two]]
    small = SETS["yz", SIGN[one], SIGN[two]]
    return [
        (big, (one, two, 0), (one, two, 1)),
        (mid, (one, 0, two), (one, 1, two)),
        (small, (0, one, two), (1, one, two)),
    ]


def slot_of(octant, d):
    place = [octant[n] + d[n] for n in range(3)]
    moved = [min(max(p // 2, -1), 1) for p in place]
    s = [p % 2 for p in place]
    return ((moved[0] + 1) * 9 + (moved[1] + 1) * 3 + moved[2] + 1) * 8 + 4 * s[0] + 2 * s[1] + s[2]


def octant_number(o):
    return 4 * o[0] + 2 * o[1] + o[2]


def fine_table():
    rows, shape = [], None
    for j in range(4):
        row, form = [], []
        for fours, first, second in jobs_of(j):
            row += [octant_number(first), octant_number(second)]
            counts = []
            for f in fours:
                row.append(f)
                counts.append(len(FOURS[f]))
                for d in FOURS[f]:
                    row += [NUMBER[d], slot_of(first, d), slot_of(second, d)]
            form.append(counts)
        assert shape is None or shape == form
        rows.append(row)
        shape = form
    return np.array(rows, np.int32), shape


FINE_TABLE, FINE_FORM = fine_table()


def coarse_table(spare):
    chunks = []
    for turn in range(PX):
        offsets = [d for d in SHIFTS if d[0] % PX == turn]
        fours = [n for n, four in enumerate(FOURS) if four[0][0] % PX == turn]
        parts = 1 if turn == 0 else 2
        cut, cut4 = -(-len(offsets) // parts), -(-len(fours) // parts)
        for part in range(parts):
            chunks.append(
                (turn, offsets[part * cut : (part + 1) * cut], fours[part * cut4 : (part + 1) * cut4])
            )
    count = max(len(c[1]) for c in chunks)
    count4 = max(len(c[2]) for c in chunks)
    count += (count + count4) % 2

    def entry(d):
        if d is None:
            return [0, spare, 24]
        return [NUMBER[d], NUMBER[d], (d[1] + 3) * 7 + d[2] + 3]

    rows = []
    for turn, offsets, fours in chunks:
        row = [turn]
        for n in range(count):
            row += entry(offsets[n] if n < len(offsets) else None)
        for n in range(count4):
            four = FOURS[fours[n]] if n < len(fours) else ()
            row.append(fours[n] if n < len(fours) else 0)
            for place in range(4):
                row += entry(four[place] if place < len(four) else None)
        rows.append(row)
    return np.array(rows, np.int32), count, count4


def rest_order(offsets):
    hot = np.zeros((offsets, 4 * LANES), np.float32)
    for n, four in enumerate(FOURS):
        for place, d in enumerate(four):
            hot[NUMBER[d], place * LANES + n] = 1
    return hot


DEPTH = 6


def main_operator_kernel(first, blocks, w, *refs):
    main, held, sems = refs[-3:]

    def copy(n):
        at = pl.multiple_of((first + n) * 8, 8)
        slot = lax.rem(n, DEPTH)
        return pltpu.make_async_copy(w.at[pl.ds(at, 8), 0:LANES, :], held.at[slot], sems.at[slot])

    for n in range(DEPTH - 1):
        copy(n).start()

    def body(n, carry):
        @pl.when(n + DEPTH - 1 < blocks)
        def _():
            copy(n + DEPTH - 1).start()

        copy(n).wait()
        at = pl.multiple_of((first + n) * 8, 8)
        main[:, pl.ds(at, 8), :] = jnp.transpose(held[lax.rem(n, DEPTH)], (2, 0, 1))
        return carry

    lax.fori_loop(0, blocks, body, 0)


def rest_operator_kernel(w, order, rest, held, sem):
    chans, _, offsets = w.shape
    left = chans - LANES
    whole = pltpu.make_async_copy(w.at[:, LANES:chans, :], held, sem)
    whole.start()
    whole.wait()

    for at in range(0, chans, 8):
        y = held[pl.ds(at, 8)].reshape(8 * left, offsets)
        y = jnp.dot(y, order[...], preferred_element_type=F32).astype(BF)
        stacked = []
        for m in range(8):
            part = padded(y[m * left : (m + 1) * left], 32)
            stacked.append(
                jnp.concatenate([part[:, f * LANES : (f + 1) * LANES] for f in range(4)], 0)
            )
        turned = jnp.transpose(jnp.stack(stacked), (2, 0, 1))
        rest[:, pl.ds(at, 8), :] = turned[0 : rest.shape[0]]


def mask_kernel(fine, hot, out):
    keep = (fine[...] >= 0).astype(F32).astype(BF)
    halves = to_octants(keep, hot[...])
    offsets = fine.shape[0]
    for s in range(8):
        out[s, 0:offsets, :] = halves[s // 4][:, (s % 4) * LANES : (s % 4 + 1) * LANES]


def shifted(tab, depth, axis, kind, step, inside, outside):
    if step == 0:
        return inside
    stride = (PY * PZ, PZ, 1)[axis]
    return roll(pick(tab, ("stage", depth, axis, kind, step), outside, inside), -step * stride)


def gathered(tab, d, kinds, done):
    axis = len(done)
    if axis == 3:
        return kinds[done]
    inside = gathered(tab, d, kinds, done + (0,))
    if d[axis] == 0:
        return inside
    return pick(tab, ("out", d, axis), gathered(tab, d, kinds, done + (1,)), inside)


def dot_pieces(pieces):
    left = jnp.concatenate([p[0] for p in pieces], 1)
    right = jnp.concatenate([p[1] for p in pieces], 0)
    return jnp.dot(left, right, preferred_element_type=F32)


def main_kernel(
    form, par, ft, ct, own, hz, hy, hyz, got_a, got_b, tab, outside, main, rest, keep, clist,
    down, inverse, hot, _slots, _plane, out, slots, plane, acc, cacc, cmask,
):
    chans = acc.shape[1]
    rows = own.shape[1]
    row = PY * PZ
    kinds = {}
    p, m = sides(par, 0, got_a[5], got_b[5])
    py, my = roll(p, LANES // 2), roll(m, LANES // 2)
    pz, mz = sides(par, 0, got_a[6], got_b[6])
    arrived = {
        (0, 0, 0): (p, m),
        (0, 1, 0): (pick(tab, "half", py, p), pick(tab, "half", m, my)),
        (0, 0, 1): (pz, mz),
        (0, 1, 1): (roll(pz, -4), roll(mz, -4)),
    }
    for k in KINDS_YZ:
        far = (1, k[1], k[2])
        kinds[far] = pick(tab, ("plus", 2, far, 0), *arrived[k])
    planes(tab, kinds, 1, plane)
    offsets = clist.shape[0]
    present = padded((clist[...] >= 0).astype(F32), cmask.shape[1])
    for turn in range(PX):
        turned = roll(present, turn * row)
        cmask[turn, :, 0:LANES] = turned * (1 - outside[...])
        cmask[turn, :, LANES:] = turned * outside[...]
    acc[...] = jnp.zeros_like(acc)
    cacc[...] = jnp.zeros_like(cacc)

    def fine_sources(s):
        block, t = s // 2, s % 2
        u, v = s % 4, s // 4
        far = (PX - 1) * row

        at_a, at_b = -8 - 64 * t, -9 - 2 * u - 64 * v
        if form[3]:
            hx = hxy = turn_by(got_a[block], at_a + far * par[0])
            hxz = hxyz = turn_by(got_a[4], at_b + far * par[0])
        else:
            p, m = sides(par, 0, got_a[block], got_b[block])
            p, m = turn_by(p, at_a), turn_by(m, at_a + far)
            hx = pick(tab, ("plus", 1, (1, 0, 0), 0), p, m)
            hxy = pick(tab, ("plus", 1, (1, 1, 0), 0), p, m)
            p, m = sides(par, 0, got_a[4], got_b[4])
            p, m = turn_by(p, at_b), turn_by(m, at_b + far)
            hxz = pick(tab, ("plus", 1, (1, 0, 1), 0), p, m)
            hxyz = pick(tab, ("plus", 1, (1, 1, 1), 0), p, m)
        kinds = {
            (0, 0, 0): own[s], (0, 1, 0): hy[s], (0, 0, 1): hz[s], (0, 1, 1): hyz[s],
            (1, 0, 0): hx, (1, 1, 0): hxy, (1, 0, 1): hxz, (1, 1, 1): hxyz,
        }
        steps = [d for d in itertools.product((-1, 0, 1), repeat=3) if d[0]]
        put_slots(tab, s, kinds, slots, steps)

    def coarse_chunk(c):
        base = c * form[2]
        turn = ct[base]

        def source(at, lo, hi):
            md, pn = ct[at + 1], ct[at + 2]
            shape = (hi - lo, 2 * LANES)
            mask = jnp.broadcast_to(cmask[turn, pl.ds(md, 1), :], shape).astype(BF)
            return plane[pn, lo:hi] * mask

        at = base + 1
        pieces = []
        for n in range(form[0]):
            pieces.append((main[ct[at]], source(at, 0, LANES)))
            at = at + 3
        for n in range(form[1]):
            four = ct[at]
            at = at + 1
            rests = []
            for place in range(4):
                rests.append(source(at, LANES, rows))
                at = at + 3
            pieces.append((rest[four], jnp.concatenate(rests, 0)))
        cacc[turn] += dot_pieces(pieces)

    chunks = ct.shape[0] // form[2]
    for s in range(chunks, 8):
        fine_sources(s)

    def both(n, carry):
        fine_sources(n)
        coarse_chunk(n)
        return carry

    lax.fori_loop(0, chunks, both, 0)

    def fine_body(j, carry):
        at = j * FINE_TABLE.shape[1]
        for counts in FINE_FORM:
            first_o, second_o = ft[at], ft[at + 1]
            at = at + 2
            pieces = []

            def flush(part):
                got = dot_pieces(part)
                acc[first_o] += got[:, 0:LANES]
                acc[second_o] += got[:, LANES:]

            for count in counts:
                four = ft[at]
                at = at + 1
                rests = []
                for n in range(count):
                    d, one, two = ft[at], ft[at + 1], ft[at + 2]
                    at = at + 3
                    x = []
                    for slot, o in ((one, first_o), (two, second_o)):
                        mask = jnp.broadcast_to(keep[o, pl.ds(d, 1), :], (rows, LANES)).astype(BF)
                        x.append(slots[slot] * mask)
                    x = jnp.concatenate(x, 1)
                    pieces.append((main[d], x[0:LANES]))
                    rests.append(x[LANES:rows])
                if count < 4:
                    rests.append(jnp.zeros((32 * (4 - count), 2 * LANES), BF))
                pieces.append((rest[four], jnp.concatenate(rests, 0)))
                while len(pieces) >= 20:
                    flush(pieces[:20])
                    pieces = pieces[20:]
            if pieces:
                flush(pieces)
        return carry

    lax.fori_loop(0, 4, fine_body, 0)
    check = jnp.zeros(cacc.shape[1:2] + (LANES,), F32)
    for turn in range(PX):
        check = check + roll(cacc[turn, :, 0:LANES] + cacc[turn, :, LANES:], -turn * row)
    local = (0.5 * check).astype(BF)
    total = []
    for s in range(8):
        spread = jnp.dot(down[s], local, preferred_element_type=F32)
        total.append((acc[s] + spread).astype(BF))
    density = jnp.dot(inverse[...], jnp.concatenate(total, 1), preferred_element_type=F32).astype(BF)
    half = 4 * LANES
    layer = BY * BZ
    for a in range(2):
        natural = lax.dot_general(
            density[:, a * half : (a + 1) * half],
            hot[...],
            (((1,), (1,)), ((), ())),
            preferred_element_type=F32,
        ).astype(BF)
        for i in range(PX):
            out[:, (2 * i + a) * layer : (2 * i + a + 1) * layer] = natural[:, i * layer : (i + 1) * layer]


VMEM = pl.BlockSpec(memory_space=pltpu.VMEM)
SMEM = pl.BlockSpec(memory_space=pltpu.SMEM)
HBM = pl.BlockSpec(memory_space=pltpu.MemorySpace.HBM)


def call(kernel, name, smem, operands, outs, limit, scratch=(), flops=0, bytes_=0, hbm=(), aliases={}):
    shapes = [jax.ShapeDtypeStruct(s, t) for s, t in outs]
    return pl.pallas_call(
        kernel,
        name=name,
        in_specs=[SMEM if n < smem else HBM if n in hbm else VMEM for n in range(len(operands))],
        out_specs=[VMEM] * len(shapes),
        out_shape=shapes,
        scratch_shapes=list(scratch),
        input_output_aliases=aliases,
        compiler_params=pltpu.CompilerParams(vmem_limit_bytes=limit),
        cost_estimate=pl.CostEstimate(flops=flops, bytes_accessed=bytes_, transcendentals=0),
    )(*[
        pltpu.with_memory_space_constraint(x, pltpu.MemorySpace.HBM) if n in hbm else x
        for n, x in enumerate(operands)
    ])


def local(
    multipole, upward_maps, transfer_maps, downward_maps, check_inverse, fine_lists, coarse_lists
):
    chans = multipole.shape[0]
    offsets = transfer_maps.shape[0]
    rows = (chans + 31) // 32 * 32
    devices = lax.axis_size("curve")
    levels = devices.bit_length() - 1
    limits = grid_counts(levels)
    position = lax.axis_index("curve")
    par = jnp.stack([position >> (2 - axis) & 1 for axis in range(3)]).astype(jnp.int32)
    hot = jnp.asarray(octant_order(), BF)
    tab = jnp.asarray(TABLE)
    row_pad = (offsets + 8) // 8 * 8

    def exchange(axis, a, b):
        got_a = lax.ppermute(a, "curve", swap_pairs(devices, levels, axis, 0))
        pairs = swap_pairs(devices, levels, axis, 1)
        got_b = lax.ppermute(b, "curve", pairs) if pairs else got_a
        return got_a, got_b

    full = ((8, rows, LANES), BF)
    one = ((rows, LANES), BF)
    own, coarse, a, b = call(
        prep_kernel, "prep", 1, (par, multipole, upward_maps, hot, tab),
        [full, one, ((2, rows, LANES), BF), ((2, rows, LANES), BF)], 16 * MIB,
        flops=10**9, bytes_=2 * MIB, hbm=(1, 2, 3, 4),
        scratch=[
            pltpu.VMEM(multipole.shape, BF),
            pltpu.VMEM(upward_maps.shape, BF),
            pltpu.VMEM(hot.shape, BF),
            pltpu.VMEM(tab.shape, F32),
            pltpu.SemaphoreType.DMA((4,)),
        ],
    )
    za, zb = exchange(2, a, b)
    rests = (len(FOURS) + 7) // 8 * 8
    turned = jnp.transpose(transfer_maps, (1, 2, 0))
    order = jnp.asarray(rest_order(offsets), BF)
    blocks = chans // 8

    def turn(first, count, *given):
        (main,) = call(
            functools.partial(main_operator_kernel, first, count), "main_operators", 0,
            (turned, *given), [((offsets, chans, LANES), BF)], 10 * MIB,
            flops=count * 25 * 10**7, bytes_=count * MIB, hbm=(0,), aliases={1: 0} if given else {},
            scratch=[
                pltpu.VMEM((DEPTH, 8, LANES, offsets), BF), pltpu.SemaphoreType.DMA((DEPTH,)),
            ],
        )
        return main

    ready = 2 * blocks // 5
    main = turn(0, ready)
    za, zb, main = lax.optimization_barrier((za, zb, main))
    hz, cz, a, b = call(
        y_kernel, "pack_y", 1, (par, own, coarse, za, zb, tab),
        [full, one, ((5, rows, LANES), BF), ((5, rows, LANES), BF)], 16 * MIB,
        flops=10**6, bytes_=2 * MIB,
    )
    ya, yb = exchange(1, a, b)
    main = turn(ready, blocks - ready, main)
    ya, yb, main = lax.optimization_barrier((ya, yb, main))
    lone = not swap_pairs(devices, levels, 0, 1)
    hy, hyz, cy, cyz, *sends = call(
        x_kernel, "pack_x", 1, (par, own, coarse, hz, cz, ya, yb, tab),
        [full, full, one, one] + [((7, rows, LANES), BF)] * (1 if lone else 2), 16 * MIB,
        flops=10**6, bytes_=2 * MIB,
    )
    xa, xb = exchange(0, sends[0], sends[-1])
    (rest,) = call(
        rest_operator_kernel, "rest_operators", 0, (turned, order), [((rests, chans, LANES), BF)],
        8 * MIB, flops=5 * 10**9, bytes_=5 * MIB, hbm=(0,),
        scratch=[pltpu.VMEM((chans, chans - LANES, offsets), BF), pltpu.SemaphoreType.DMA],
    )

    early = [((216, rows, LANES), BF), ((49, rows, 2 * LANES), BF)]
    slots, plane = call(
        early_kernel, "early", 0, (own, hz, hy, hyz, coarse, cz, cy, cyz, tab), early, 8 * MIB,
        flops=10**9, bytes_=8 * MIB,
    )
    (keep,) = call(
        mask_kernel, "masks", 0, (fine_lists, hot), [((8, row_pad, LANES), F32)], 16 * MIB,
        flops=10**9, bytes_=2 * MIB,
    )
    xa, xb, slots, plane, keep, rest = lax.optimization_barrier((xa, xb, slots, plane, keep, rest))
    ft = jnp.asarray(FINE_TABLE.reshape(-1))
    table, count, count4 = coarse_table(row_pad - 1)
    beyond = [TABLE[MASKS.rows["stage", 2, 0, (0, 0, 0), d[0]]] for d in SHIFTS]
    outside = jnp.asarray(np.stack(beyond + [0 * beyond[0]] * (row_pad - offsets)))
    ct = jnp.asarray(table.reshape(-1))
    out, _, _ = call(
        functools.partial(main_kernel, (count, count4, table.shape[1], lone)), "translate", 3,
        (par, ft, ct, own, hz, hy, hyz, xa, xb, tab, outside, main, rest, keep,
         coarse_lists, downward_maps, check_inverse, hot, slots, plane),
        [((chans, multipole.shape[1]), BF), *early],
        14 * MIB, aliases={18: 1, 19: 2},
        scratch=[
            pltpu.VMEM((8, chans, LANES), F32),
            pltpu.VMEM((PX, chans, 2 * LANES), F32),
            pltpu.VMEM((PX, row_pad, 2 * LANES), F32),
        ],
        flops=2 * 10**10, bytes_=20 * MIB,
    )
    return out


def solution(mesh):
    placed = (P(None, "curve"), P(), P(), P(), P(), P(None, "curve"), P(None, "curve"))
    return jax.shard_map(
        local, mesh=mesh, in_specs=placed, out_specs=P(None, "curve"), check_vma=False
    )
```

```python
import functools
import itertools

import jax
import jax.numpy as jnp
import numpy as np
from jax import lax
from jax.experimental import pallas as pl
from jax.experimental.pallas import tpu as pltpu
from jax.sharding import PartitionSpec as P

BX, BY, BZ = 8, 8, 16
PX, PY, PZ = BX // 2, BY // 2, BZ // 2
LANES = PX * PY * PZ
EXT = (PX, PY, PZ)
BF = jnp.bfloat16
F32 = jnp.float32
SHIFTS = [
    d for d in itertools.product(range(-3, 4), repeat=3) if max(abs(d[0]), abs(d[1]), abs(d[2])) >= 2
]
NUMBER = {d: n for n, d in enumerate(SHIFTS)}
MIB = 1 << 20


def grid_counts(levels):
    return (2 ** (levels // 3), 2 ** ((levels + 1) // 3), 2 ** ((levels + 2) // 3))


def decode(position, levels):
    coords = [0, 0, 0]
    for bit_place in range(levels):
        coords[2 - bit_place % 3] += (position >> bit_place & 1) << (bit_place // 3)
    return coords


def encode(coords, levels):
    number = 0
    for bit_place in range(levels):
        number += (coords[2 - bit_place % 3] >> (bit_place // 3) & 1) << bit_place
    return number


def swap_pairs(devices, levels, axis, odd):
    pairs = []
    for number in range(devices):
        coords = decode(number, levels)
        if coords[axis] % 2 == odd and coords[axis] + 1 < grid_counts(levels)[axis]:
            coords[axis] += 1
            other = encode(coords, levels)
            pairs += [(number, other), (other, number)]
    return pairs


def lane_of(e):
    return (e[0] * PY * PZ + e[1] * PZ + e[2]) % LANES


def coords_of(axis, outside, depth):
    if outside:
        return list(range(-depth, 0)) + list(range(EXT[axis], EXT[axis] + depth))
    return list(range(EXT[axis]))


def elements(kind, depth):
    return itertools.product(*[coords_of(axis, kind[axis], depth) for axis in range(3)])


class Masks:
    def __init__(self):
        self.rows = {}
        self.table = []

    def add(self, name, lanes):
        row = np.zeros(LANES, np.float32)
        row[sorted(lanes)] = 1
        self.rows[name] = len(self.table)
        self.table.append(row)


KINDS_YZ = [(0, 0, 0), (0, 1, 0), (0, 0, 1), (0, 1, 1)]
ALL_KINDS = [tuple(k) for k in itertools.product((0, 1), repeat=3)]


def build_masks():
    masks = Masks()
    every = range(LANES)
    for depth in (1, 2):
        reach = 1 if depth == 1 else 3
        for kind in ALL_KINDS:
            for axis in range(3):
                if kind[axis]:
                    masks.add(
                        ("plus", depth, kind, axis),
                        {lane_of(e) for e in elements(kind, depth) if e[axis] >= EXT[axis]},
                    )
        for axis in range(3):
            kinds = {0: KINDS_YZ, 1: [(0, 0, 0), (0, 0, 1)], 2: [(0, 0, 0)]}[axis]
            for kind in kinds:
                for step in range(-reach, reach + 1):
                    lanes = set()
                    for e in elements(kind, depth):
                        moved = list(e)
                        moved[axis] += step
                        if not 0 <= moved[axis] < EXT[axis]:
                            lanes.add(lane_of(moved))
                    masks.add(("stage", depth, axis, kind, step), lanes)
    for d in itertools.product((-1, 0, 1), repeat=3):
        for axis in range(3):
            lanes = set()
            for e in itertools.product(*map(range, EXT)):
                moved = [e[n] + d[n] for n in range(3)]
                if not 0 <= moved[axis] < EXT[axis]:
                    lanes.add(lane_of(moved))
            if d[axis]:
                masks.add(("out", d, axis), lanes)
    for s in range(8):
        masks.add(("zpack", s), {l for l in every if l % PZ == s})
    row = PY * PZ
    for t in range(PY):
        masks.add(("ypack", t), {l for l in every if l // PZ % PY == t})
    masks.add(("xsrc_a", 0), set(range(row)))
    masks.add(("xsrc_a", 1), set(range(LANES - row, LANES)))
    for side, i in ((0, 0), (1, PX - 1)):
        masks.add(("xsrc_b", side), {lane_of((i, j, k)) for j in range(PY) for k in (-1, PZ)})
    for side, i in ((0, (0, 1)), (1, (PX - 2, PX - 1))):
        masks.add(
            ("cy", side),
            {lane_of((n, j, k)) for n in i for j in (-2, -1, PY, PY + 1) for k in range(PZ)},
        )
    masks.add("half", {l for l in every if l < LANES // 2})
    masks.add("mid", {l for l in every if 2 <= l % PZ < 6})
    for t in range(2):
        masks.add(("xpack_a", t), {l for l in every if l // 64 == t})
    for t in range(8):
        u, v = t % 4, t // 4
        masks.add(("xpack_b", t), {l for l in every if l // 64 == v and l % 8 in (2 * u, 2 * u + 1)})
    return masks


MASKS = build_masks()
TABLE = np.stack(MASKS.table)


def pick(tab, name, yes, no):
    n = MASKS.rows[name]
    row = jnp.broadcast_to(tab[n : n + 1, :], yes.shape).astype(BF)
    return jnp.where(row > 0, yes, no)


def pick_row(tab, n, yes, no):
    row = jnp.broadcast_to(tab[pl.ds(n, 1), :], yes.shape).astype(BF)
    return jnp.where(row > 0, yes, no)


def turn_by(x, by):
    return pltpu.roll(x, lax.rem(by + 4 * LANES, LANES), 1)


def roll(x, by):
    by = by % LANES
    return x if by == 0 else pltpu.roll(x, by, 1)


def padded(x, rows):
    return jnp.concatenate([x, jnp.zeros((rows - x.shape[0], x.shape[1]), x.dtype)], 0)


def octant_order():
    size = PX * BY * BZ
    row = lax.broadcasted_iota(jnp.int32, (size, 1), 0)
    column = lax.broadcasted_iota(jnp.int32, (size, size), 1)
    i, y, z = row // (BY * BZ), row // BZ % BY, row % BZ
    place = (2 * (y % 2) + z % 2) * LANES + i * PY * PZ + (y // 2) * PZ + z // 2
    return jnp.where(column == place, 1.0, 0.0).astype(BF)


def to_octants(x, hot):
    layer = BY * BZ
    halves = []
    for a in range(2):
        chunk = jnp.concatenate(
            [x[:, (2 * i + a) * layer : (2 * i + a + 1) * layer] for i in range(PX)], 1
        )
        halves.append(jnp.dot(chunk, hot, preferred_element_type=F32))
    return halves


def prep_kernel(
    par, mult_hbm, up_hbm, tab_hbm, own, coarse, send_a, send_b, hot, mult, up, tab, sems
):
    copies = [
        pltpu.make_async_copy(src, dst, sems.at[n])
        for n, (src, dst) in enumerate(
            ((mult_hbm, mult), (tab_hbm, tab), (up_hbm, up))
        )
    ]
    for copy in copies:
        copy.start()
    chans = mult.shape[0]
    rows = own.shape[1]
    hot[...] = octant_order()
    copies[0].wait()
    copies[1].wait()
    halves = to_octants(mult[...], hot[...])
    copies[2].wait()
    total = jnp.zeros((chans, LANES), F32)
    pack = [[None] * 2, [None] * 2]
    for s in range(8):
        x = halves[s // 4][:, (s % 4) * LANES : (s % 4 + 1) * LANES].astype(BF)
        total = total + jnp.dot(up[s], x, preferred_element_type=F32)
        x = padded(x, rows)
        own[s] = x
        block, t = s // PY, s % PY
        for side in range(2):
            moved = roll(x, PZ * (t - (PY - 1) * side))
            pack[side][block] = (
                moved if t == 0 else pick(tab, ("ypack", t), moved, pack[side][block])
            )
    c = padded(total.astype(BF), rows)
    coarse[...] = c
    even = par[1] == 0
    for block in range(2):
        send_a[block] = jnp.where(even, pack[1][block], pack[0][block])
        send_b[block] = jnp.where(even, pack[0][block], pack[1][block])
    send_a[2] = c
    send_b[2] = c


def sides(par, axis, got_a, got_b):
    even = par[axis] == 0
    plus = jnp.where(even, got_a, got_b)
    minus = jnp.where(even, got_b, got_a)
    return plus, minus


def z_kernel(par, own, coarse, got_a, got_b, tab, hy, cy, send_a, send_b):
    row = PY * PZ
    for s in range(8):
        block, t = s // PY, s % PY
        p, m = sides(par, 1, got_a[block], got_b[block])
        hy[s] = pick(
            tab, ("plus", 1, (0, 1, 0), 1), roll(p, row - PZ * t), roll(m, -PZ - PZ * t)
        )
    p, m = sides(par, 1, got_a[2], got_b[2])
    far = pick(tab, ("plus", 2, (0, 1, 0), 1), roll(p, row), roll(m, -row))
    cy[...] = far
    even = par[2] == 0
    for n, ref in ((0, own), (1, hy)):
        pack = [None, None]
        for s in range(8):
            for side in range(2):
                moved = roll(ref[s], s - (PZ - 1) * side)
                pack[side] = moved if s == 0 else pick(tab, ("zpack", s), moved, pack[side])
        send_a[n] = jnp.where(even, pack[1], pack[0])
        send_b[n] = jnp.where(even, pack[0], pack[1])
    for send in (send_a, send_b):
        send[2] = coarse[...]
        send[3] = far


def x_kernel(par, own, coarse, hy, cy, got_a, got_b, tab, hz, hyz, cz, cyz, *sends):
    row = PY * PZ
    for n, ref, kind in ((0, hz, (0, 0, 1)), (1, hyz, (0, 1, 1))):
        p, m = sides(par, 2, got_a[n], got_b[n])
        for s in range(8):
            ref[s] = pick(tab, ("plus", 1, kind, 2), roll(p, PZ - s), roll(m, -1 - s))
    for n, ref, kind in ((2, cz, (0, 0, 1)), (3, cyz, (0, 1, 1))):
        p, m = sides(par, 2, got_a[n], got_b[n])
        ref[...] = pick(tab, ("plus", 2, kind, 2), roll(p, PZ), roll(m, -PZ))
    near = [cy[...], cyz[...]]
    half = LANES // 2
    other = roll(near[0], half)
    low = pick(tab, "half", coarse[...], pick(tab, ("cy", 0), near[0], other))
    high = pick(tab, "half", pick(tab, ("cy", 1), near[0], other), coarse[...])
    edges = pick(tab, "mid", roll(near[1], 4), cz[...])
    for send, odd in zip(sends, (0, 1)):
        side = par[0] if odd else 1 - par[0]
        far = (PX - 1) * row * side
        whole, line = [None] * 4, None
        for s in range(8):
            block, t = s // 2, s % 2
            u, v = s % 4, s // 4
            a = pick_row(tab, MASKS.rows["xsrc_a", 0] + side, own[s], hy[s])
            b = pick_row(tab, MASKS.rows["xsrc_b", 0] + side, hz[s], hyz[s])
            a = turn_by(a, 8 + 64 * t - far)
            b = turn_by(b, 9 + 2 * u + 64 * v - far)
            whole[block] = a if t == 0 else pick(tab, ("xpack_a", t), a, whole[block])
            line = b if s == 0 else pick(tab, ("xpack_b", s), b, line)
        for block in range(4):
            send[block] = whole[block]
        send[4] = line
        send[5] = jnp.where(side == 1, high, low)
        send[6] = edges


def planes(tab, kinds, far, plane):
    for dy in range(-3, 4):
        y = {
            z: shifted(tab, 2, 1, (0, 0, z), dy, kinds[far, 0, z], kinds[far, 1, z])
            for z in (0, 1)
        }
        for dz in range(-3, 4):
            plane[(dy + 3) * 7 + dz + 3, :, far * LANES : (far + 1) * LANES] = shifted(
                tab, 2, 2, (0, 0, 0), dz, y[0], y[1]
            )


def put_slots(tab, s, kinds, slots, steps):
    for d in steps:
        n = ((d[0] + 1) * 9 + (d[1] + 1) * 3 + d[2] + 1) * 8 + s
        by = d[0] * PY * PZ + d[1] * PZ + d[2]
        slots[n] = roll(gathered(tab, d, kinds, ()), -by)


def early_kernel(own, hz, hy, hyz, coarse, cz, cy, cyz, tab, slots, plane):
    kinds = {(0, 0, 0): coarse[...], (0, 1, 0): cy[...], (0, 0, 1): cz[...], (0, 1, 1): cyz[...]}
    planes(tab, kinds, 0, plane)
    steps = [(0, dy, dz) for dy in (-1, 0, 1) for dz in (-1, 0, 1) if dy or dz]

    def body(s, carry):
        kinds = {(0, 0, 0): own[s], (0, 1, 0): hy[s], (0, 0, 1): hz[s], (0, 1, 1): hyz[s]}
        put_slots(tab, s, kinds, slots, steps)
        return carry

    lax.fori_loop(0, 8, body, 0)


def offset_sets():
    fours = []

    def add(offsets):
        start = len(fours)
        for turn in range(PX):
            like = [d for d in offsets if d[0] % PX == turn]
            for n in range(0, len(like), 4):
                fours.append(tuple(like[n : n + 4]))
        return list(range(start, len(fours)))

    small = range(-2, 3)
    sets = {}
    sets["free"] = add([d for d in SHIFTS if max(map(abs, d)) == 2])
    for axis in range(3):
        for sign in (-3, 3):
            sets[axis, sign] = add(
                [d for d in SHIFTS if d[axis] == sign and all(abs(d[o]) <= 2 for o in range(3) if o != axis)]
            )
    for sx in (-3, 3):
        for sy in (-3, 3):
            sets["xy", sx, sy] = add([(sx, sy, z) for z in small])
        for sz in (-3, 3):
            sets["xz", sx, sz] = add([(sx, y, sz) for y in small])
    for sy in (-3, 3):
        for sz in (-3, 3):
            sets["yz", sy, sz] = add([(x, sy, sz) for x in range(-3, 4)])
    return fours, sets


FOURS, SETS = offset_sets()
SIGN = (3, -3)


def jobs_of(j):
    one, two = j // 2, j % 2
    big = SETS["free"] + SETS[0, SIGN[one]] + SETS[1, SIGN[two]] + SETS["xy", SIGN[one], SIGN[two]]
    mid = SETS[2, SIGN[two]] + SETS["xz", SIGN[one], SIGN[two]]
    small = SETS["yz", SIGN[one], SIGN[two]]
    return [
        (big, (one, two, 0), (one, two, 1)),
        (mid, (one, 0, two), (one, 1, two)),
        (small, (0, one, two), (1, one, two)),
    ]


def slot_of(octant, d):
    place = [octant[n] + d[n] for n in range(3)]
    moved = [min(max(p // 2, -1), 1) for p in place]
    s = [p % 2 for p in place]
    return ((moved[0] + 1) * 9 + (moved[1] + 1) * 3 + moved[2] + 1) * 8 + 4 * s[0] + 2 * s[1] + s[2]


def octant_number(o):
    return 4 * o[0] + 2 * o[1] + o[2]


def rest_order(offsets):
    hot = np.zeros((offsets, 4 * LANES), np.float32)
    for n, four in enumerate(FOURS):
        for place, d in enumerate(four):
            hot[NUMBER[d], place * LANES + n] = 1
    return hot


DEPTH = 6


def main_operator_kernel(first, blocks, w, *refs):
    main, held, sems = refs[-3:]

    def copy(n):
        at = pl.multiple_of((first + n) * 8, 8)
        slot = lax.rem(n, DEPTH)
        return pltpu.make_async_copy(w.at[pl.ds(at, 8), 0:LANES, :], held.at[slot], sems.at[slot])

    for n in range(DEPTH - 1):
        copy(n).start()

    def body(n, carry):
        @pl.when(n + DEPTH - 1 < blocks)
        def _():
            copy(n + DEPTH - 1).start()

        copy(n).wait()
        at = pl.multiple_of((first + n) * 8, 8)
        main[:, pl.ds(at, 8), :] = jnp.transpose(held[lax.rem(n, DEPTH)], (2, 0, 1))
        return carry

    lax.fori_loop(0, blocks, body, 0)


def rest_operator_kernel(w, order, rest, held, sem):
    chans, _, offsets = w.shape
    left = chans - LANES
    whole = pltpu.make_async_copy(w.at[:, LANES:chans, :], held, sem)
    whole.start()
    whole.wait()

    for at in range(0, chans, 8):
        y = held[pl.ds(at, 8)].reshape(8 * left, offsets)
        y = jnp.dot(y, order[...], preferred_element_type=F32).astype(BF)
        stacked = []
        for m in range(8):
            part = padded(y[m * left : (m + 1) * left], 32)
            stacked.append(
                jnp.concatenate([part[:, f * LANES : (f + 1) * LANES] for f in range(4)], 0)
            )
        turned = jnp.transpose(jnp.stack(stacked), (2, 0, 1))
        rest[:, pl.ds(at, 8), :] = turned[0 : rest.shape[0]]


def mask_kernel(fine, hot, out):
    keep = (fine[...] >= 0).astype(F32).astype(BF)
    halves = to_octants(keep, hot[...])
    offsets = fine.shape[0]
    for s in range(8):
        out[s, 0:offsets, :] = halves[s // 4][:, (s % 4) * LANES : (s % 4 + 1) * LANES]


def shifted(tab, depth, axis, kind, step, inside, outside):
    if step == 0:
        return inside
    stride = (PY * PZ, PZ, 1)[axis]
    return roll(pick(tab, ("stage", depth, axis, kind, step), outside, inside), -step * stride)


def gathered(tab, d, kinds, done):
    axis = len(done)
    if axis == 3:
        return kinds[done]
    inside = gathered(tab, d, kinds, done + (0,))
    if d[axis] == 0:
        return inside
    return pick(tab, ("out", d, axis), gathered(tab, d, kinds, done + (1,)), inside)


def dot_pieces(pieces):
    left = jnp.concatenate([p[0] for p in pieces], 1)
    right = jnp.concatenate([p[1] for p in pieces], 0)
    return jnp.dot(left, right, preferred_element_type=F32)


GROUP = 24


def main_kernel(
    lone, par, own, hz, hy, hyz, got_a, got_b, tab, outside, main, rest, keep, clist,
    down, inverse, hot, _slots, _plane, out, slots, plane, acc, cacc, cmask,
):
    chans = acc.shape[1]
    rows = own.shape[1]
    row = PY * PZ
    kinds = {}
    p, m = sides(par, 0, got_a[5], got_b[5])
    py, my = roll(p, LANES // 2), roll(m, LANES // 2)
    pz, mz = sides(par, 0, got_a[6], got_b[6])
    arrived = {
        (0, 0, 0): (p, m),
        (0, 1, 0): (pick(tab, "half", py, p), pick(tab, "half", m, my)),
        (0, 0, 1): (pz, mz),
        (0, 1, 1): (roll(pz, -4), roll(mz, -4)),
    }
    for k in KINDS_YZ:
        far = (1, k[1], k[2])
        kinds[far] = pick(tab, ("plus", 2, far, 0), *arrived[k])
    planes(tab, kinds, 1, plane)
    offsets = clist.shape[0]
    present = padded((clist[...] >= 0).astype(F32), cmask.shape[1])
    for turn in range(PX):
        turned = roll(present, turn * row)
        cmask[turn, :, 0:LANES] = turned * (1 - outside[...])
        cmask[turn, :, LANES:] = turned * outside[...]
    acc[...] = jnp.zeros_like(acc)
    cacc[...] = jnp.zeros_like(cacc)

    def fine_sources(s):
        block, t = s // 2, s % 2
        u, v = s % 4, s // 4
        far = (PX - 1) * row

        at_a, at_b = -8 - 64 * t, -9 - 2 * u - 64 * v
        if lone:
            hx = hxy = turn_by(got_a[block], at_a + far * par[0])
            hxz = hxyz = turn_by(got_a[4], at_b + far * par[0])
        else:
            p, m = sides(par, 0, got_a[block], got_b[block])
            p, m = turn_by(p, at_a), turn_by(m, at_a + far)
            hx = pick(tab, ("plus", 1, (1, 0, 0), 0), p, m)
            hxy = pick(tab, ("plus", 1, (1, 1, 0), 0), p, m)
            p, m = sides(par, 0, got_a[4], got_b[4])
            p, m = turn_by(p, at_b), turn_by(m, at_b + far)
            hxz = pick(tab, ("plus", 1, (1, 0, 1), 0), p, m)
            hxyz = pick(tab, ("plus", 1, (1, 1, 1), 0), p, m)
        kinds = {
            (0, 0, 0): own[s], (0, 1, 0): hy[s], (0, 0, 1): hz[s], (0, 1, 1): hyz[s],
            (1, 0, 0): hx, (1, 1, 0): hxy, (1, 0, 1): hxz, (1, 1, 1): hxyz,
        }
        steps = [d for d in itertools.product((-1, 0, 1), repeat=3) if d[0]]
        put_slots(tab, s, kinds, slots, steps)

    def source(d, lo, hi):
        n = NUMBER[d]
        mask = jnp.broadcast_to(cmask[d[0] % PX, n : n + 1, :], (hi - lo, 2 * LANES)).astype(BF)
        return plane[(d[1] + 3) * 7 + d[2] + 3, lo:hi] * mask

    def whole(d):
        return main[NUMBER[d]], source(d, 0, LANES)

    def quarters(n):
        parts = [source(d, LANES, rows) for d in FOURS[n]]
        if len(parts) < 4:
            parts.append(jnp.zeros((32 * (4 - len(parts)), 2 * LANES), BF))
        return rest[n], jnp.concatenate(parts, 0)

    groups = []
    for turn in range(PX):
        makers = [functools.partial(whole, d) for d in SHIFTS if d[0] % PX == turn]
        makers += [
            functools.partial(quarters, n) for n, four in enumerate(FOURS) if four[0][0] % PX == turn
        ]
        parts = -(-len(makers) // GROUP)
        size = -(-len(makers) // (2 * parts)) * 2
        groups += [(turn, makers[n : n + size]) for n in range(0, len(makers), size)]
    done = 0
    for n, (turn, makers) in enumerate(groups):
        while done < 8 and done * len(groups) <= 8 * n:
            fine_sources(done)
            done += 1
        cacc[turn] += dot_pieces([make() for make in makers])

    for j in range(4):
        for fours, first, second in jobs_of(j):
            first_o, second_o = octant_number(first), octant_number(second)
            pieces = []

            def flush(part):
                got = dot_pieces(part)
                acc[first_o] += got[:, 0:LANES]
                acc[second_o] += got[:, LANES:]

            for four in fours:
                rests = []
                for d in FOURS[four]:
                    n = NUMBER[d]
                    x = []
                    for octant, o in ((first, first_o), (second, second_o)):
                        mask = jnp.broadcast_to(keep[o, n : n + 1, :], (rows, LANES)).astype(BF)
                        x.append(slots[slot_of(octant, d)] * mask)
                    x = jnp.concatenate(x, 1)
                    pieces.append((main[n], x[0:LANES]))
                    rests.append(x[LANES:rows])
                if len(rests) < 4:
                    rests.append(jnp.zeros((32 * (4 - len(rests)), 2 * LANES), BF))
                pieces.append((rest[four], jnp.concatenate(rests, 0)))
                while len(pieces) >= GROUP:
                    flush(pieces[:GROUP])
                    pieces = pieces[GROUP:]
            if pieces:
                flush(pieces)
    check = jnp.zeros(cacc.shape[1:2] + (LANES,), F32)
    for turn in range(PX):
        check = check + roll(cacc[turn, :, 0:LANES] + cacc[turn, :, LANES:], -turn * row)
    local = (0.5 * check).astype(BF)
    total = []
    for s in range(8):
        spread = jnp.dot(down[s], local, preferred_element_type=F32)
        total.append((acc[s] + spread).astype(BF))
    density = jnp.dot(inverse[...], jnp.concatenate(total, 1), preferred_element_type=F32).astype(BF)
    half = 4 * LANES
    layer = BY * BZ
    for a in range(2):
        natural = lax.dot_general(
            density[:, a * half : (a + 1) * half],
            hot[...],
            (((1,), (1,)), ((), ())),
            preferred_element_type=F32,
        ).astype(BF)
        for i in range(PX):
            out[:, (2 * i + a) * layer : (2 * i + a + 1) * layer] = natural[:, i * layer : (i + 1) * layer]


VMEM = pl.BlockSpec(memory_space=pltpu.VMEM)
SMEM = pl.BlockSpec(memory_space=pltpu.SMEM)
HBM = pl.BlockSpec(memory_space=pltpu.MemorySpace.HBM)


def call(kernel, name, smem, operands, outs, limit, scratch=(), flops=0, bytes_=0, hbm=(), aliases={}):
    shapes = [jax.ShapeDtypeStruct(s, t) for s, t in outs]
    return pl.pallas_call(
        kernel,
        name=name,
        in_specs=[SMEM if n < smem else HBM if n in hbm else VMEM for n in range(len(operands))],
        out_specs=[VMEM] * len(shapes),
        out_shape=shapes,
        scratch_shapes=list(scratch),
        input_output_aliases=aliases,
        compiler_params=pltpu.CompilerParams(vmem_limit_bytes=limit),
        cost_estimate=pl.CostEstimate(flops=flops, bytes_accessed=bytes_, transcendentals=0),
    )(*[
        pltpu.with_memory_space_constraint(x, pltpu.MemorySpace.HBM) if n in hbm else x
        for n, x in enumerate(operands)
    ])


def local(
    multipole, upward_maps, transfer_maps, downward_maps, check_inverse, fine_lists, coarse_lists
):
    chans = multipole.shape[0]
    offsets = transfer_maps.shape[0]
    rows = (chans + 31) // 32 * 32
    devices = lax.axis_size("curve")
    levels = devices.bit_length() - 1
    limits = grid_counts(levels)
    position = lax.axis_index("curve")
    par = jnp.stack([position >> (2 - axis) & 1 for axis in range(3)]).astype(jnp.int32)
    tab = jnp.asarray(TABLE)
    row_pad = (offsets + 8) // 8 * 8

    def exchange(axis, a, b):
        got_a = lax.ppermute(a, "curve", swap_pairs(devices, levels, axis, 0))
        pairs = swap_pairs(devices, levels, axis, 1)
        got_b = lax.ppermute(b, "curve", pairs) if pairs else got_a
        return got_a, got_b

    full = ((8, rows, LANES), BF)
    one = ((rows, LANES), BF)
    side = PX * BY * BZ
    own, coarse, a, b, hot = call(
        prep_kernel, "prep", 1, (par, multipole, upward_maps, tab),
        [full, one, ((3, rows, LANES), BF), ((3, rows, LANES), BF), ((side, side), BF)], 16 * MIB,
        flops=10**9, bytes_=2 * MIB, hbm=(1, 2, 3),
        scratch=[
            pltpu.VMEM(multipole.shape, BF),
            pltpu.VMEM(upward_maps.shape, BF),
            pltpu.VMEM(tab.shape, F32),
            pltpu.SemaphoreType.DMA((3,)),
        ],
    )
    ya, yb = exchange(1, a, b)
    rests = (len(FOURS) + 7) // 8 * 8
    turned = jnp.transpose(transfer_maps, (1, 2, 0))
    order = jnp.asarray(rest_order(offsets), BF)
    blocks = chans // 8

    def turn(first, count, *given):
        (main,) = call(
            functools.partial(main_operator_kernel, first, count), "main_operators", 0,
            (turned, *given), [((offsets, chans, LANES), BF)], 10 * MIB,
            flops=count * 25 * 10**7, bytes_=count * MIB, hbm=(0,), aliases={1: 0} if given else {},
            scratch=[
                pltpu.VMEM((DEPTH, 8, LANES, offsets), BF), pltpu.SemaphoreType.DMA((DEPTH,)),
            ],
        )
        return main

    ready = 3 * blocks // 5
    main = turn(0, ready)
    ya, yb, main = lax.optimization_barrier((ya, yb, main))
    hy, cy, a, b = call(
        z_kernel, "pack_z", 1, (par, own, coarse, ya, yb, tab),
        [full, one, ((4, rows, LANES), BF), ((4, rows, LANES), BF)], 16 * MIB,
        flops=10**6, bytes_=2 * MIB,
    )
    za, zb = exchange(2, a, b)
    main = turn(ready, blocks - ready, main)
    za, zb, main = lax.optimization_barrier((za, zb, main))
    lone = not swap_pairs(devices, levels, 0, 1)
    hz, hyz, cz, cyz, *sends = call(
        x_kernel, "pack_x", 1, (par, own, coarse, hy, cy, za, zb, tab),
        [full, full, one, one] + [((7, rows, LANES), BF)] * (1 if lone else 2), 16 * MIB,
        flops=10**6, bytes_=2 * MIB,
    )
    xa, xb = exchange(0, sends[0], sends[-1])
    (rest,) = call(
        rest_operator_kernel, "rest_operators", 0, (turned, order), [((rests, chans, LANES), BF)],
        8 * MIB, flops=5 * 10**9, bytes_=5 * MIB, hbm=(0,),
        scratch=[pltpu.VMEM((chans, chans - LANES, offsets), BF), pltpu.SemaphoreType.DMA],
    )

    early = [((216, rows, LANES), BF), ((49, rows, 2 * LANES), BF)]
    slots, plane = call(
        early_kernel, "early", 0, (own, hz, hy, hyz, coarse, cz, cy, cyz, tab), early, 8 * MIB,
        flops=10**9, bytes_=8 * MIB,
    )
    (keep,) = call(
        mask_kernel, "masks", 0, (fine_lists, hot), [((8, row_pad, LANES), F32)], 16 * MIB,
        flops=10**9, bytes_=2 * MIB,
    )
    xa, xb, slots, plane, keep, rest = lax.optimization_barrier((xa, xb, slots, plane, keep, rest))
    beyond = [TABLE[MASKS.rows["stage", 2, 0, (0, 0, 0), d[0]]] for d in SHIFTS]
    outside = jnp.asarray(np.stack(beyond + [0 * beyond[0]] * (row_pad - offsets)))
    out, _, _ = call(
        functools.partial(main_kernel, lone), "translate", 1,
        (par, own, hz, hy, hyz, xa, xb, tab, outside, main, rest, keep,
         coarse_lists, downward_maps, check_inverse, hot, slots, plane),
        [((chans, multipole.shape[1]), BF), *early],
        14 * MIB, aliases={16: 1, 17: 2},
        scratch=[
            pltpu.VMEM((8, chans, LANES), F32),
            pltpu.VMEM((PX, chans, 2 * LANES), F32),
            pltpu.VMEM((PX, row_pad, 2 * LANES), F32),
        ],
        flops=2 * 10**10, bytes_=20 * MIB,
    )
    return out


def solution(mesh):
    placed = (P(None, "curve"), P(), P(), P(), P(), P(None, "curve"), P(None, "curve"))
    return jax.shard_map(
        local, mesh=mesh, in_specs=placed, out_specs=P(None, "curve"), check_vma=False
    )
```
